256 devices in a mesh: dp: 16 (over z, x_hi), tensor: 16 (over x_lo, y, core).
Axes of the slice: x: 4 (x_hi: 2, x_lo: 2; x = x_hi * 2 + x_lo), y: 4, z: 8, core: 2. Of those that a mesh axis runs over, the one named last changes fastest.
Arguments:
- inputs: bfloat16 [8192, 2304], P(('dp', 'tensor')), may hold values from -6 to 6
- out_grad: bfloat16 [8192, 2304], P(('dp', 'tensor')), may hold values from -0.59765625 to 0.59765625
- gate_pre: bfloat16 [8192, 18432], P('dp', 'tensor'), may hold values from -6 to 6
- up_pre: bfloat16 [8192, 18432], P('dp', 'tensor'), may hold values from -6 to 6
- w_down: bfloat16 [18432, 2304], P('tensor'), may hold values from -0.046875 to 0.046875
- proj_new: bfloat16 [2304, 3, 256], replicated, may hold values from -0.125 to 0.125
- proj_old: bfloat16 [2304, 3, 256], P('tensor'), may hold values from -0.125 to 0.125
- first_old: float32 [256, 3, 18432], P('dp', None, 'tensor'), may hold values from -6 to 6
- second_old: float32 [256, 3, 18432], P('dp', None, 'tensor'), may hold values from 0.1 to 10
Outputs:
- first_new: float32 [256, 3, 18432], P('dp', None, 'tensor')
- second_new: float32 [256, 3, 18432], P('dp', None, 'tensor')
The draws below stay inside these ranges and needn't reach their ends.
All inputs are finite; a program needn't handle non-finite values.
Results may differ from the reference program's by a relative error of at most 0.0005.
Values may be sent and summed in bfloat16 or wider, within the bound.
A program may use at most 64 MiB of HBM per device.

```python
import math
import jax
import jax.numpy as jnp
from jax import lax

D = 2304
FF = 18432
RANK = 256
TOK_DEV = 32
TOKENS = 8192
N_DP = 16
N_TENSOR = 16


def block_scale(rng, extent, split, smallest, high):
    gain = 1.0
    for axis_at, parts in split:
        steps = jax.random.uniform(jax.random.fold_in(jax.random.fold_in(rng, 6), axis_at), (parts,), jnp.float32, smallest / len(split), high / len(split))
        gain = gain * jnp.repeat(jnp.exp(steps), extent[axis_at] // parts).reshape((-1,) + (1,) * (len(extent) - 1 - axis_at))
    return gain


def centred(stream_key, shape, spread, bound, cuts=(), dtype=jnp.bfloat16):
    drawn = spread * jax.random.normal(stream_key, shape, jnp.float32)
    if cuts:
        drawn = drawn * block_scale(stream_key, shape, cuts, -0.22, 0.18)
    return jnp.clip(drawn, -bound, bound).astype(dtype)


def setup_inputs(seed: int = 0) -> dict:
    key_list = jax.random.split(jax.random.key(seed), 10)
    inputs = centred(key_list[0], (TOKENS, D), 1.0, 6.0, ((0, 256),))
    out_grad = centred(key_list[1], (TOKENS, D), 0.1, 0.59765625, ((0, 256),))
    gate_pre = centred(key_list[2], (TOKENS, FF), 1.0, 6.0, ((0, 16), (1, 16)))
    up_pre = centred(key_list[3], (TOKENS, FF), 1.0, 6.0, ((0, 16), (1, 16)))
    w_down = centred(key_list[4], (FF, D), FF ** -0.5, 0.046875, ((0, 16),))
    proj_new = centred(key_list[5], (D, 3, RANK), D ** -0.5, 0.125)
    proj_old = centred(key_list[6], (D, 3, RANK), D ** -0.5, 0.125, ((0, 16),))
    first_old = centred(key_list[7], (RANK, 3, FF), 1.0, 6.0, ((0, 16), (2, 16)), jnp.float32)
    second_old = jnp.clip(jnp.exp(math.log(10.0) - 4.6051702 * jax.random.uniform(key_list[8], (RANK, 3, FF), jnp.float32) ** block_scale(key_list[8], (RANK, 3, FF), ((0, 16), (2, 16)), -0.2, 0.2)), 0.1, 10.0)
    return dict(inputs=inputs, out_grad=out_grad, gate_pre=gate_pre, up_pre=up_pre, w_down=w_down, proj_new=proj_new, proj_old=proj_old, first_old=first_old, second_old=second_old)


coeff = 0.7978845608028654


def gelu_pair(gate):
    inner = coeff * (gate + 0.044715 * gate * gate * gate)
    tval = jnp.tanh(inner)
    value = 0.5 * gate * (1.0 + tval)
    slope = 0.5 * (1.0 + tval) + 0.5 * gate * (1.0 - tval * tval) * coeff * (1.0 + 3.0 * 0.044715 * gate * gate)
    return value, slope


def reference(inputs, out_grad, gate_pre, up_pre, w_down, proj_new, proj_old, first_old, second_old):
    flat = proj_new.reshape(D, 3 * RANK)
    in_proj = jnp.dot(inputs, flat[:, :2 * RANK], preferred_element_type=jnp.float32).astype(jnp.bfloat16)
    out_proj = jnp.dot(out_grad, flat[:, 2 * RANK:], preferred_element_type=jnp.float32).astype(jnp.bfloat16)
    group = TOK_DEV * N_TENSOR

    def step(carry, blocks):
        dy_b, gate_b, up_b, xp_b, yp_b = blocks
        hidden_grad = jnp.dot(dy_b, w_down.T, preferred_element_type=jnp.float32)
        value, slope = gelu_pair(gate_b.astype(jnp.float32))
        upf = up_b.astype(jnp.float32)
        gate_grad = (hidden_grad * upf * slope).astype(jnp.bfloat16)
        up_grad = (hidden_grad * value).astype(jnp.bfloat16)
        hidden = (value * upf).astype(jnp.bfloat16)
        low_gate = jnp.dot(xp_b[:, :RANK].T, gate_grad, preferred_element_type=jnp.float32)
        low_up = jnp.dot(xp_b[:, RANK:].T, up_grad, preferred_element_type=jnp.float32)
        low_down = jnp.dot(yp_b.T, hidden, preferred_element_type=jnp.float32)
        return carry + jnp.stack([low_gate, low_up, low_down], axis=1), None

    blocks = (out_grad.reshape(N_DP, group, D), gate_pre.reshape(N_DP, group, FF),
              up_pre.reshape(N_DP, group, FF), in_proj.reshape(N_DP, group, 2 * RANK),
              out_proj.reshape(N_DP, group, RANK))
    low_grad, unused = lax.scan(step, jnp.zeros((RANK, 3, FF), jnp.float32), blocks)
    rotation = jnp.einsum('dki,dkj->kij', proj_new.astype(jnp.float32), proj_old.astype(jnp.float32),
                          precision=lax.Precision.HIGHEST)
    turned_first = jnp.einsum('kij,jkc->ikc', rotation, first_old, precision=lax.Precision.HIGHEST)
    turned_second = jnp.einsum('kij,jkc->ikc', rotation * rotation, second_old, precision=lax.Precision.HIGHEST)
    first_new = 0.9 * turned_first + 0.1 * low_grad
    second_new = 0.999 * turned_second + 0.001 * low_grad * low_grad
    return first_new, second_new
```

```python
import jax
import jax.numpy as jnp
from jax import lax
from jax.experimental import pallas as pl
from jax.experimental.pallas import tpu as pltpu
from jax.sharding import PartitionSpec as P

coeff = 0.7978845608028654
F32 = jnp.float32
BF16 = jnp.bfloat16
D = 2304
C = 1152
TOK = 512
SH = 32
RANK = 256
SLAB = 144
CH = 384
QT0 = (0, 9, 15, 21)
QN = (9, 6, 6, 6)
TOP = 32768.0
MESH = pl.DeviceIdType.MESH


def enc(x, buf):
    n, rows, _ = x.shape
    top = jnp.max(jnp.max(jnp.abs(x), axis=0, keepdims=True), axis=1, keepdims=True)
    top = jnp.broadcast_to(jnp.maximum(top, 1e-30), (1, rows, 128)).astype(BF16)
    buf[pl.ds(n, 1)] = top
    u = x * (TOP / top.astype(F32))
    u2 = u * u
    u4 = u2 * u2
    buf[pl.ds(0, n)] = ((u4 * u2) * (u * jnp.abs(u))).astype(BF16)


def dec(buf, n):
    v = buf[pl.ds(0, n)].astype(F32)
    r = jnp.exp2(jnp.log2(jnp.abs(v)) * 0.125)
    scale = buf[pl.ds(n, 1)].astype(F32) * (1.0 / TOP)
    return jnp.where(v < 0.0, -r, r) * scale


def kernel(
    inp_h, og_h, gate_h, up_h, w_h, pn_h, po_h, fo_h, so_h,
    of_ref, os_ref,
    inp, Y, Pb, old, gate, up, w, pn, V, U, G, H, GG, UG, L, R, M, T, TB, FIN, LOW,
    lsend, lrecv, ssend, srecv, xsend, xrecv,
    ld, gs, gr, ms, mr, ts, tr, ls, lr, ss, sr, xs, xr,
):
    d = lax.axis_index("dp")
    t = lax.axis_index("tensor")
    z = d // 2
    xh = lax.rem(d, 2)
    c = lax.rem(t, 2)
    y = lax.rem(t // 2, 4)
    xl = t // 8
    kd = jnp.minimum(d // 5, 2)

    def tid(a, b):
        return a * 8 + b * 2 + c

    yn = lax.rem(y + 1, 4)
    yb = lax.rem(y + 3, 4)
    y2 = lax.rem(y + 2, 4)
    xo = 1 - xl
    sib = t + 1 - 2 * c
    xp = tid(xo, y)
    yp = tid(xl, yn)
    ym = tid(xl, yb)
    zn = lax.rem(z + 1, 8)
    zb = lax.rem(z + 7, 8)
    zlong = jnp.where(c == 0, zn, zb)
    zshort = jnp.where(c == 0, zb, zn)
    dlong = zlong * 2 + xh
    dshort = zshort * 2 + xh
    dx = d + 1 - 2 * xh
    step = 1 - 2 * c

    def loc(src, dst, i):
        return pltpu.make_async_copy(src, dst, ld.at[i])

    own = pl.ds(pl.multiple_of(t * SH, SH), SH)
    loads = [
        loc(og_h, Y.at[own], 0),
        loc(inp_h, inp, 1),
        loc(pn_h, pn, 2),
        loc(po_h.at[kd], old.at[pl.ds(pl.multiple_of(t * SLAB, 16), SLAB)], 3),
        loc(gate_h, gate, 4),
        loc(up_h, up, 5),
        loc(w_h, w, 6),
    ]
    for a in loads:
        a.start()

    bar = pltpu.get_barrier_semaphore()
    for peer in (sib, xp, yp, ym):
        pl.semaphore_signal(bar, inc=1, device_id={"tensor": peer}, device_id_type=MESH)

    @pl.loop(1, 16)
    def _(j):
        pl.semaphore_signal(
            bar, inc=1, device_id={"dp": lax.rem(d + j, 16)}, device_id_type=MESH
        )

    for a in loads[:3]:
        a.wait()
    for k in range(3):
        lhs = inp[...] if k < 2 else Y[own, :]
        Pb[own, k * RANK : (k + 1) * RANK] = jnp.dot(
            lhs, pn[k], preferred_element_type=F32
        ).astype(BF16)
    loads[3].wait()
    pl.semaphore_wait(bar, 19)

    pay = ((Pb, SH, SH), (Y, SH, SH), (old, SLAB, 16))

    def gcopy(p, slot, target, i):
        buf, rows, mult = pay[p]
        sl = pl.ds(pl.multiple_of(slot * rows, mult), rows)
        return pltpu.make_async_remote_copy(
            src_ref=buf.at[sl], dst_ref=buf.at[sl], send_sem=gs.at[p, i],
            recv_sem=gr.at[p, slot], device_id={"tensor": target}, device_id_type=MESH,
        )

    def gsend(p, slot, target, i):
        gcopy(p, slot, target, i).start()

    def gwait(p, slot):
        gcopy(p, slot, sib, 0).wait_recv()

    def g0(p):
        gsend(p, t, xp, 0)
        gsend(p, t, yp, 1)
        gsend(p, t, ym, 2)
        gsend(p, t, sib, 3)

    dfrom = jnp.where(c == 0, ym, yp)
    dto = jnp.where(c == 0, yp, ym)

    def g1(p):
        gwait(p, xp)
        gsend(p, xp, yp, 4)
        gsend(p, xp, ym, 5)
        gsend(p, xp, sib, 6)
        gwait(p, ym)
        gwait(p, yp)
        gsend(p, dfrom, dto, 7)
        gsend(p, ym, sib, 8)
        gsend(p, yp, sib, 9)

    def g2(p):
        far = tid(xl, y2)
        gwait(p, far)
        gsend(p, far, xp, 12)
        gsend(p, far, sib, 13)
        gwait(p, tid(xo, yb))
        gsend(p, tid(xo, yb), sib, 10)
        gwait(p, tid(xo, yn))
        gsend(p, tid(xo, yn), sib, 11)
        gwait(p, tid(xo, y2))
        gsend(p, tid(xo, y2), sib, 14)

    def g3(p):
        @pl.loop(0, 8)
        def _(j):
            gwait(p, j * 2 + 1 - c)

    def colof(e):
        return pl.multiple_of(jnp.minimum(e * 256, 896), 128)

    def mrem(m, o, src):
        return pltpu.make_async_remote_copy(
            src_ref=src, dst_ref=M.at[m, pl.ds(pl.multiple_of(d * 16, 16), 16)],
            send_sem=ms.at[m, o], recv_sem=mr.at[m, d],
            device_id={"dp": o}, device_id_type=MESH,
        )

    def msend():
        @pl.loop(0, 15)
        def _(o):
            for m, ref in enumerate((fo_h, so_h)):
                src = ref.at[o // 5, :, pl.ds(colof(lax.rem(o, 5)), 256)]

                @pl.when(o != d)
                def _():
                    mrem(m, o, src).start()

                @pl.when(o == d)
                def _():
                    pltpu.make_async_copy(
                        src, M.at[m, pl.ds(pl.multiple_of(d * 16, 16), 16)], mr.at[m, d]
                    ).start()

    def trem(m, dst, o):
        return pltpu.make_async_remote_copy(
            src_ref=T.at[m, pl.ds(pl.multiple_of(dst * 16, 16), 16)], dst_ref=TB.at[m, o],
            send_sem=ts.at[m, dst], recv_sem=tr.at[m, o],
            device_id={"dp": dst}, device_id_type=MESH,
        )

    def turn():
        R[...] = lax.dot_general(
            pn[kd], old[...], (((0,), (0,)), ((), ())), preferred_element_type=F32
        )

        @pl.when(d < 15)
        def _():
            @pl.loop(0, 16)
            def _(s):
                for m in range(2):
                    pltpu.make_async_copy(
                        M.at[m, pl.ds(pl.multiple_of(s * 16, 16), 16)],
                        M.at[m, pl.ds(pl.multiple_of(s * 16, 16), 16)], mr.at[m, s]
                    ).wait()

            rot = R[...]
            for m in range(2):
                T[m] = jnp.dot(
                    rot if m == 0 else rot * rot, M[m],
                    precision=lax.Precision.HIGHEST, preferred_element_type=F32,
                )

            @pl.loop(0, 16)
            def _(j):
                for m in range(2):
                    @pl.when(j != d)
                    def _():
                        trem(m, j, d).start()

                    @pl.when(j == d)
                    def _():
                        pltpu.make_async_copy(
                            T.at[m, pl.ds(pl.multiple_of(d * 16, 16), 16)], TB.at[m, d],
                            tr.at[m, d],
                        ).start()

    def lcopy(q, r):
        n = QN[q] + 1
        t0 = QT0[q] + q
        return pltpu.make_async_remote_copy(
            src_ref=lsend.at[r, pl.ds(t0, n)], dst_ref=lrecv.at[r, pl.ds(t0, n)],
            send_sem=ls.at[q, r], recv_sem=lr.at[q, r],
            device_id={"dp": dlong}, device_id_type=MESH,
        )

    def scopy(q, r):
        n = QN[q] + 1
        t0 = QT0[q] + q
        return pltpu.make_async_remote_copy(
            src_ref=ssend.at[r, pl.ds(t0, n)], dst_ref=srecv.at[r, pl.ds(t0, n)],
            send_sem=ss.at[q, r], recv_sem=sr.at[q, r],
            device_id={"dp": dshort}, device_id_type=MESH,
        )

    def mine(q, zdest):
        return L[pl.ds(QT0[q], QN[q]), pl.ds(pl.multiple_of(zdest * 32, 32), 32), :]

    def rnd(q, r):
        n = QN[q]
        tiles = pl.ds(QT0[q] + q, n + 1)
        x = mine(q, lax.rem(z + 8 + step * (4 - r), 8))
        if r > 0:
            lcopy(q, r - 1).wait_recv()
            x = x + dec(lrecv.at[r - 1, tiles], n)
        enc(x, lsend.at[r, tiles])
        lcopy(q, r).start()
        if r < 3:
            x = mine(q, lax.rem(z + 8 - step * (3 - r), 8))
            if r > 0:
                scopy(q, r - 1).wait_recv()
                x = x + dec(srecv.at[r - 1, tiles], n)
            enc(x, ssend.at[r, tiles])
            scopy(q, r).start()

    def xcopy(q):
        n = QN[q] + 1
        t0 = QT0[q] + q
        return pltpu.make_async_remote_copy(
            src_ref=xsend.at[pl.ds(t0, n)], dst_ref=xrecv.at[pl.ds(t0, n)],
            send_sem=xs.at[q], recv_sem=xr.at[q],
            device_id={"dp": dx}, device_id_type=MESH,
        )

    def fin(q):
        n = QN[q]
        tiles = pl.ds(QT0[q] + q, n + 1)
        dst = pl.ds(QT0[q], n)
        lcopy(q, 3).wait_recv()
        scopy(q, 2).wait_recv()
        FIN[dst] = mine(q, z) + dec(lrecv.at[3, tiles], n) + dec(srecv.at[2, tiles], n)
        enc(FIN[dst, pl.ds(pl.multiple_of((1 - xh) * 16, 16), 16), :], xsend.at[tiles])
        xcopy(q).start()

    def last(q):
        n = QN[q]
        tiles = pl.ds(QT0[q] + q, n + 1)
        dst = pl.ds(QT0[q], n)
        xcopy(q).wait_recv()
        LOW[dst] = FIN[dst, pl.ds(pl.multiple_of(xh * 16, 16), 16), :] + dec(xrecv.at[tiles], n)

    g0(0)
    g0(1)
    g1(0)
    g1(1)
    msend()
    g0(2)
    loads[4].wait()
    loads[5].wait()

    def act(lo, hi):
        @pl.loop(lo, hi)
        def _(i):
            rows = pl.ds(pl.multiple_of(i * 16, 16), 16)
            g = gate[rows, :].astype(F32)
            u = up[rows, :].astype(F32)
            g2_ = g * g
            tv = jnp.tanh(coeff * (g + 0.044715 * (g2_ * g)))
            val = 0.5 * g * (1.0 + tv)
            slope = 0.5 * (1.0 + tv) + 0.5 * g * (1.0 - tv * tv) * (
                coeff * (1.0 + 3.0 * 0.044715 * g2_)
            )
            V[rows, :] = val
            U[rows, :] = u * slope
            G[rows, :] = (val * u).astype(BF16)

    act(0, 16)
    g2(0)
    g2(1)
    act(16, 32)
    g3(0)

    contract = (((0,), (0,)), ((), ()))
    for j in range(3):
        r = lax.dot_general(
            Pb[:, 2 * RANK : 3 * RANK], G[:, j * CH : (j + 1) * CH], contract,
            preferred_element_type=F32,
        )
        for i in range(3):
            L[3 * j + i] = r[:, i * 128 : (i + 1) * 128]
    rnd(0, 0)
    g1(2)
    g3(1)
    loads[6].wait()

    def chunk(j):
        cols = slice(j * CH, (j + 1) * CH)
        H[...] = lax.dot_general(
            Y[...], w[cols, :], (((1,), (1,)), ((), ())), preferred_element_type=F32
        )

        @pl.loop(0, 16)
        def _(i):
            rows = pl.ds(pl.multiple_of(i * 32, 32), 32)
            h = H[rows, :]
            GG[rows, :] = (h * U[rows, cols]).astype(BF16)
            UG[rows, :] = (h * V[rows, cols]).astype(BF16)

        for k, ref in enumerate((GG, UG)):
            r = lax.dot_general(
                Pb[:, k * RANK : (k + 1) * RANK], ref[...], contract, preferred_element_type=F32
            )
            for i in range(3):
                L[9 + 6 * j + 3 * k + i] = r[:, i * 128 : (i + 1) * 128]

    chunk(0)
    rnd(0, 1)
    rnd(1, 0)
    g2(2)
    chunk(1)
    rnd(0, 2)
    rnd(1, 1)
    rnd(2, 0)
    chunk(2)
    rnd(0, 3)
    rnd(1, 2)
    rnd(2, 1)
    rnd(3, 0)
    g3(2)
    turn()
    fin(0)
    rnd(1, 3)
    rnd(2, 2)
    rnd(3, 1)
    last(0)
    fin(1)
    rnd(2, 3)
    rnd(3, 2)
    last(1)
    fin(2)
    rnd(3, 3)
    last(2)

    @pl.loop(0, 15)
    def _(o):
        for m in range(2):
            pltpu.make_async_copy(TB.at[m, o], TB.at[m, o], tr.at[m, o]).wait()

    def out(q):
        for i in range(QN[q]):
            if q == 0:
                k, ct = 2, i
            else:
                k, ct = i // 3, (q - 1) * 3 + i % 3
            e, off = (4, 128) if ct == 8 else (ct // 2, (ct % 2) * 128)
            low = LOW[QT0[q] + i]
            tf = TB[0, 5 * k + e, :, off : off + 128]
            tsq = TB[1, 5 * k + e, :, off : off + 128]
            cols = slice(ct * 128, (ct + 1) * 128)
            of_ref[k, :, cols] = 0.9 * tf + 0.1 * low
            os_ref[k, :, cols] = 0.999 * tsq + 0.001 * low * low

    for q in range(3):
        out(q)
    fin(3)
    last(3)
    out(3)

    for p in range(3):
        for i in range(15):
            gcopy(p, t, sib, i).wait_send()

    @pl.loop(0, 15)
    def _(o):
        for m in range(2):
            @pl.when(o != d)
            def _():
                mrem(m, o, fo_h.at[0, :, pl.ds(0, 256)]).wait_send()

    @pl.when(d < 15)
    def _():
        @pl.loop(0, 16)
        def _(j):
            for m in range(2):
                @pl.when(j != d)
                def _():
                    trem(m, j, d).wait_send()

    for q in range(4):
        for r in range(4):
            lcopy(q, r).wait_send()
        for r in range(3):
            scopy(q, r).wait_send()
        xcopy(q).wait_send()


def on_device(inputs, out_grad, gate_pre, up_pre, w_down, proj_new, proj_old, first_old, second_old):
    flip = lambda a: jnp.transpose(a, (1, 0, 2))
    shape = jax.ShapeDtypeStruct((3, 16, C), F32)
    dma = pltpu.SemaphoreType.DMA
    first, second = pl.pallas_call(
        kernel,
        out_shape=(shape, shape),
        in_specs=[pl.BlockSpec(memory_space=pl.ANY)] * 9,
        out_specs=(pl.BlockSpec(memory_space=pltpu.VMEM),) * 2,
        scratch_shapes=[
            pltpu.VMEM((SH, D), BF16),
            pltpu.VMEM((TOK, D), BF16),
            pltpu.VMEM((TOK, 3 * RANK), BF16),
            pltpu.VMEM((D, RANK), BF16),
            pltpu.VMEM((TOK, C), BF16),
            pltpu.VMEM((TOK, C), BF16),
            pltpu.VMEM((C, D), BF16),
            pltpu.VMEM((3, D, RANK), BF16),
            pltpu.VMEM((TOK, C), F32),
            pltpu.VMEM((TOK, C), F32),
            pltpu.VMEM((TOK, C), BF16),
            pltpu.VMEM((TOK, CH), F32),
            pltpu.VMEM((TOK, CH), BF16),
            pltpu.VMEM((TOK, CH), BF16),
            pltpu.VMEM((27, RANK, 128), F32),
            pltpu.VMEM((RANK, RANK), F32),
            pltpu.VMEM((2, RANK, RANK), F32),
            pltpu.VMEM((2, RANK, RANK), F32),
            pltpu.VMEM((2, 15, 16, 256), F32),
            pltpu.VMEM((27, 32, 128), F32),
            pltpu.VMEM((27, 16, 128), F32),
            pltpu.VMEM((4, 31, 32, 128), BF16),
            pltpu.VMEM((4, 31, 32, 128), BF16),
            pltpu.VMEM((3, 31, 32, 128), BF16),
            pltpu.VMEM((3, 31, 32, 128), BF16),
            pltpu.VMEM((31, 16, 128), BF16),
            pltpu.VMEM((31, 16, 128), BF16),
            dma((7,)), dma((3, 15)), dma((3, 16)),
            dma((2, 16)), dma((2, 16)), dma((2, 16)), dma((2, 16)),
            dma((4, 4)), dma((4, 4)), dma((4, 3)), dma((4, 3)), dma((4,)), dma((4,)),
        ],
        compiler_params=pltpu.CompilerParams(
            collective_id=0, has_side_effects=True, vmem_limit_bytes=63 * 1024 * 1024
        ),
    )(
        inputs, out_grad, gate_pre, up_pre, w_down, flip(proj_new), flip(proj_old),
        flip(first_old), flip(second_old),
    )
    return flip(first), flip(second)


def solution(mesh):
    placed = (
        P(("dp", "tensor"), None),
        P(("dp", "tensor"), None),
        P("dp", "tensor"),
        P("dp", "tensor"),
        P("tensor", None),
        P(),
        P("tensor", None, None),
        P("dp", None, "tensor"),
        P("dp", None, "tensor"),
    )
    return jax.shard_map(
        on_device,
        mesh=mesh,
        in_specs=placed,
        out_specs=(P("dp", None, "tensor"), P("dp", None, "tensor")),
        check_vma=False,
    )
```

```python
import jax
import jax.numpy as jnp
from jax import lax
from jax.experimental import pallas as pl
from jax.experimental.pallas import tpu as pltpu
from jax.sharding import PartitionSpec as P

coeff = 0.7978845608028654
F32 = jnp.float32
BF16 = jnp.bfloat16
D = 2304
C = 1152
TOK = 512
SH = 32
RANK = 256
SLAB = 144
CH = 384
QT0 = (0, 5, 9, 15, 21)
QN = (5, 4, 6, 6, 6)
NQ = 5
ROWS = 27 * 32 + 8 * NQ
XROWS = 27 * 16 + 8 * NQ
BACK = (0, 2, 1, 3, 5, 4, 6)
TOP = 32768.0
MESH = pl.DeviceIdType.MESH


def top_of(x):
    top = jnp.max(jnp.max(jnp.abs(x), axis=0), axis=0, keepdims=True)
    return jnp.broadcast_to(jnp.maximum(top, 1e-30), (8, 128)).astype(BF16)


def code(x, top):
    n, rows, _ = x.shape
    u = x * (TOP / top.astype(F32))[0:1][None]
    u2 = u * u
    u4 = u2 * u2
    return ((u4 * u2) * (u * jnp.abs(u))).astype(BF16).reshape(n * rows, 128)


def value(v, scale, n):
    v = v.astype(F32)
    r = jnp.exp2(jnp.log2(jnp.abs(v)) * 0.125)
    return (jnp.where(v < 0.0, -r, r) * (scale * (1.0 / TOP))).reshape(n, -1, 128)


def enc(x, buf):
    n, rows, _ = x.shape
    top = top_of(x)
    buf[pl.ds(n * rows, 8)] = top
    buf[pl.ds(0, n * rows)] = code(x, top)


def dec(buf, n, rows):
    scale = buf[pl.ds(n * rows, 8)].astype(F32)[0:1]
    return value(buf[pl.ds(0, n * rows)], scale, n)


def enc2(a, b, buf):
    ta, tb = top_of(a), top_of(b)
    first = lax.broadcasted_iota(jnp.int32, (8, 128), 0) < 4
    buf[pl.ds(64, 8)] = jnp.where(first, ta.astype(F32), tb.astype(F32)).astype(BF16)
    buf[pl.ds(0, 32)] = code(a, ta)
    buf[pl.ds(32, 32)] = code(b, tb)


def dec2(buf):
    scale = buf[pl.ds(64, 8)].astype(F32)
    return value(buf[pl.ds(0, 32)], scale[0:1], 2), value(buf[pl.ds(32, 32)], scale[4:5], 2)


def kernel(
    inp_h, og_h, gate_h, up_h, w_h, pn_h, po_h, fo_h, so_h,
    low_h, tf_h, ts_h,
    inp, Y, Pb, old, gate, up, w, pn, fo, so, V, U, G, H, GG, UG, L, R, M, T, MS, MR, TS, TB, FIN, OUT,
    rsend, rrecv, xsend, xrecv,
    ld, gs, gr, ms, mr, ts, tr, rs, rr, xs, xr,
):
    d = lax.axis_index("dp")
    t = lax.axis_index("tensor")
    z = d // 2
    xh = lax.rem(d, 2)
    c = lax.rem(t, 2)
    y = lax.rem(t // 2, 4)
    xl = t // 8
    kd = jnp.minimum(d // 5, 2)

    def tid(a, b):
        return a * 8 + b * 2 + c

    yn = lax.rem(y + 1, 4)
    yb = lax.rem(y + 3, 4)
    y2 = lax.rem(y + 2, 4)
    xo = 1 - xl
    sib = t + 1 - 2 * c
    xp = tid(xo, y)
    yp = tid(xl, yn)
    ym = tid(xl, yb)
    zn = lax.rem(z + 1, 8)
    zb = lax.rem(z + 7, 8)
    zlong = jnp.where(c == 0, zn, zb)
    zshort = jnp.where(c == 0, zb, zn)
    dlong = zlong * 2 + xh
    dshort = zshort * 2 + xh
    dx = d + 1 - 2 * xh
    step = 1 - 2 * c

    def loc(src, dst, i):
        return pltpu.make_async_copy(src, dst, ld.at[i])

    own = pl.ds(pl.multiple_of(t * SH, SH), SH)
    loads = [
        loc(og_h, Y.at[own], 0),
        loc(inp_h, inp, 1),
        loc(pn_h, pn, 2),
        loc(po_h.at[kd], old.at[pl.ds(pl.multiple_of(t * SLAB, 16), SLAB)], 3),
        loc(gate_h, gate, 4),
        loc(up_h, up, 5),
        loc(w_h, w, 6),
        loc(fo_h, fo, 7),
        loc(so_h, so, 8),
    ]
    for i in (1, 0, 2, 7, 8, 3):
        loads[i].start()

    bar = pltpu.get_barrier_semaphore()
    lane = (xp, yp, ym, tid(xl, y2), tid(xo, yn), tid(xo, yb), tid(xo, y2))
    for peer in (sib,) + lane:
        pl.semaphore_signal(bar, inc=1, device_id={"tensor": peer}, device_id_type=MESH)

    @pl.loop(1, 16)
    def _(j):
        pl.semaphore_signal(
            bar, inc=1, device_id={"dp": lax.rem(d + j, 16)}, device_id_type=MESH
        )

    pay = ((Pb, SH, SH), (Y, SH, SH), (old, SLAB, 16))

    def gcopy(p, slot, target, i):
        buf, rows, mult = pay[p]
        sl = pl.ds(pl.multiple_of(slot * rows, mult), rows)
        return pltpu.make_async_remote_copy(
            src_ref=buf.at[sl], dst_ref=buf.at[sl], send_sem=gs.at[p],
            recv_sem=gr.at[p, i], device_id={"tensor": target}, device_id_type=MESH,
        )

    def gsend(p, slot, target, i):
        gcopy(p, slot, target, i).start()

    def gwait(p, j):
        gcopy(p, lane[j], sib, j).wait_recv()

    def shards(p, n, sem):
        buf, rows, _ = pay[p]
        part = buf.at[pl.ds(0, n * rows)]
        pltpu.make_async_copy(part, part, sem).wait()

    def project():
        for a in loads[:3]:
            a.wait()
        for i in (4, 5, 6):
            loads[i].start()
        for k in range(3):
            lhs = inp[...] if k < 2 else Y[own, :]
            Pb[own, k * RANK : (k + 1) * RANK] = jnp.dot(
                lhs, pn[k], preferred_element_type=F32
            ).astype(BF16)

    def gown(p, n):
        for j in range(n):
            gsend(p, t, lane[j], BACK[j])
        gsend(p, t, sib, 7)

    def gmirror(p, js):
        for j in js:
            gwait(p, j)
            gsend(p, lane[j], sib, 7)

    def gpair(p):
        gwait(p, 0)
        gsend(p, xp, yp, 5)
        gsend(p, xp, ym, 4)
        gsend(p, xp, sib, 7)

    def gfar(p):
        gwait(p, 3)
        gsend(p, lane[3], xp, 6)
        gsend(p, lane[3], sib, 7)

    def g3(p):
        shards(p, 8, gr.at[p, 7])

    def mrem(o):
        return pltpu.make_async_remote_copy(
            src_ref=MS.at[o], dst_ref=MR.at[d], send_sem=ms, recv_sem=mr,
            device_id={"dp": o}, device_id_type=MESH,
        )

    def menc():
        loads[7].wait()
        loads[8].wait()
        for o in range(15):
            c0 = min((o % 5) * 256, 896)
            pair = [
                jnp.stack([ref[o // 5, :, c0 + i * 128 : c0 + i * 128 + 128] for i in range(2)])
                for ref in (fo, so)
            ]
            enc2(*pair, MS.at[o])

    def msend(par):
        @pl.loop(0, 8)
        def _(j):
            o = 2 * j + par

            @pl.when(jnp.logical_and(o < 15, o != d))
            def _():
                mrem(o).start()

            @pl.when(jnp.logical_and(o < 15, o == d))
            def _():
                pltpu.make_async_copy(MS.at[o], MR.at[d], mr).start()

    def trem(dst):
        return pltpu.make_async_remote_copy(
            src_ref=TS.at[dst], dst_ref=TB.at[d], send_sem=ts, recv_sem=tr,
            device_id={"dp": dst}, device_id_type=MESH,
        )

    def turn():
        R[...] = lax.dot_general(
            pn[kd], old[...], (((0,), (0,)), ((), ())), preferred_element_type=F32
        )

        @pl.when(d < 15)
        def _():
            pltpu.make_async_copy(MR, MR, mr).wait()

            @pl.loop(0, 16)
            def _(s):
                rows = pl.ds(pl.multiple_of(s * 16, 16), 16)
                for m, x in enumerate(dec2(MR.at[s])):
                    M[m, rows, 0:128] = x[0]
                    M[m, rows, 128:256] = x[1]

            rot = R[...]
            for m in range(2):
                T[m] = jnp.dot(
                    rot if m == 0 else rot * rot, M[m],
                    precision=lax.Precision.HIGHEST, preferred_element_type=F32,
                )

            @pl.loop(0, 16)
            def _(j):
                rows = pl.ds(pl.multiple_of(j * 16, 16), 16)
                pair = [jnp.stack([T[m, rows, 0:128], T[m, rows, 128:256]]) for m in range(2)]
                enc2(*pair, TS.at[j])

                @pl.when(j != d)
                def _():
                    trem(j).start()

                @pl.when(j == d)
                def _():
                    pltpu.make_async_copy(TS.at[j], TB.at[d], tr).start()

    def span(q, rows=32):
        return pl.ds(QT0[q] * rows + 8 * q, QN[q] * rows + 8)

    def rcopy(q, i):
        sp = span(q)
        return pltpu.make_async_remote_copy(
            src_ref=rsend.at[i, sp], dst_ref=rrecv.at[i, sp], send_sem=rs, recv_sem=rr.at[q, i],
            device_id={"dp": dlong if i < 4 else dshort}, device_id_type=MESH,
        )

    def mine(q, zdest):
        return L[pl.ds(QT0[q], QN[q]), pl.ds(pl.multiple_of(zdest * 32, 32), 32), :]

    def rnd(q, r):
        n = QN[q]
        tiles = span(q)
        for i, far in ((r, step * (4 - r)), (4 + r, -step * (3 - r))):
            if i == 7:
                continue
            x = mine(q, lax.rem(z + 8 + far, 8))
            if r > 0:
                rcopy(q, i - 1).wait_recv()
                x = x + dec(rrecv.at[i - 1, tiles], n, 32)
            enc(x, rsend.at[i, tiles])
            rcopy(q, i).start()

    def xcopy(q):
        sp = span(q, 16)
        return pltpu.make_async_remote_copy(
            src_ref=xsend.at[sp], dst_ref=xrecv.at[sp], send_sem=xs, recv_sem=xr.at[q],
            device_id={"dp": dx}, device_id_type=MESH,
        )

    def fin(q):
        n = QN[q]
        tiles = span(q)
        dst = pl.ds(QT0[q], n)
        rcopy(q, 3).wait_recv()
        rcopy(q, 6).wait_recv()
        FIN[dst] = mine(q, z) + dec(rrecv.at[3, tiles], n, 32) + dec(rrecv.at[6, tiles], n, 32)
        enc(FIN[dst, pl.ds(pl.multiple_of((1 - xh) * 16, 16), 16), :], xsend.at[span(q, 16)])
        xcopy(q).start()

    def last(q):
        n = QN[q]
        dst = pl.ds(QT0[q], n)
        xcopy(q).wait_recv()
        low = FIN[dst, pl.ds(pl.multiple_of(xh * 16, 16), 16), :] + dec(xrecv.at[span(q, 16)], n, 16)
        for i in range(n):
            g = QT0[q] + i
            k, ct = (2, g) if g < 9 else ((g - 9) % 6 // 3, (g - 9) // 6 * 3 + (g - 9) % 3)
            OUT[k, :, ct * 128 : (ct + 1) * 128] = low[i]
        if q < 2:
            part = (2, slice(None), pl.ds(QT0[q] * 128, n * 128))
        else:
            part = (pl.ds(0, 2), slice(None), pl.ds((q - 2) * CH, CH))
        pltpu.make_async_copy(OUT.at[part], low_h.at[part], ld.at[9]).start()

    def back():
        pltpu.make_async_copy(TB, TB, tr).wait()
        for o in range(15):
            for m, x in enumerate(dec2(TB.at[o])):
                for i in range(2):
                    ct = min(2 * (o % 5), 7) + i
                    if o % 5 < 4 or i == 1:
                        OUT[3 + 3 * m + o // 5, :, ct * 128 : (ct + 1) * 128] = x[i]
        loc(OUT.at[pl.ds(3, 3)], tf_h, 9).start()
        loc(OUT.at[pl.ds(6, 3)], ts_h, 9).start()

    project()
    pl.semaphore_wait(bar, 23)
    gown(0, 7)
    gown(1, 4)
    menc()
    msend(xh)
    loads[4].wait()
    loads[5].wait()

    def act(lo, hi):
        @pl.loop(lo, hi)
        def _(i):
            rows = pl.ds(pl.multiple_of(i * 16, 16), 16)
            g = gate[rows, :].astype(F32)
            u = up[rows, :].astype(F32)
            g2_ = g * g
            tv = jnp.tanh(coeff * (g + 0.044715 * (g2_ * g)))
            val = 0.5 * g * (1.0 + tv)
            slope = 0.5 * (1.0 + tv) + 0.5 * g * (1.0 - tv * tv) * (
                coeff * (1.0 + 3.0 * 0.044715 * g2_)
            )
            V[rows, :] = val
            U[rows, :] = u * slope
            G[rows, :] = (val * u).astype(BF16)

    contract = (((0,), (0,)), ((), ()))

    def lowd():
        for j in range(3):
            r = lax.dot_general(
                Pb[:, 2 * RANK : 3 * RANK], G[:, j * CH : (j + 1) * CH], contract,
                preferred_element_type=F32,
            )
            for i in range(3):
                L[3 * j + i] = r[:, i * 128 : (i + 1) * 128]

    def chunk(j):
        cols = slice(j * CH, (j + 1) * CH)
        H[...] = lax.dot_general(
            Y[...], w[cols, :], (((1,), (1,)), ((), ())), preferred_element_type=F32
        )

        @pl.loop(0, 16)
        def _(i):
            rows = pl.ds(pl.multiple_of(i * 32, 32), 32)
            h = H[rows, :]
            GG[rows, :] = (h * U[rows, cols]).astype(BF16)
            UG[rows, :] = (h * V[rows, cols]).astype(BF16)

        for k, ref in enumerate((GG, UG)):
            r = lax.dot_general(
                Pb[:, k * RANK : (k + 1) * RANK], ref[...], contract, preferred_element_type=F32
            )
            for i in range(3):
                L[9 + 6 * j + 3 * k + i] = r[:, i * 128 : (i + 1) * 128]

    def gdrain():
        for p in range(3):
            shards(p, 15, gs.at[p])

    def mdrain():
        @pl.when(d < 15)
        def _():
            part = MS.at[pl.ds(0, 14)]
            pltpu.make_async_copy(part, part, ms).wait()
            part = TS.at[pl.ds(0, 15)]
            pltpu.make_async_copy(part, part, ts).wait()

        @pl.when(d == 15)
        def _():
            pltpu.make_async_copy(MS, MS, ms).wait()

    def rdrain():
        pltpu.make_async_copy(rsend, rsend, rs).wait()
        pltpu.make_async_copy(xsend, xsend, xs).wait()
        pltpu.make_async_copy(OUT, OUT, ld.at[9]).wait()

    act(0, 32)
    gmirror(0, range(7))
    gpair(1)
    msend(1 - xh)
    g3(0)
    lowd()
    rnd(0, 0)
    rnd(1, 0)
    gfar(1)
    loads[3].wait()
    gown(2, 4)
    gmirror(1, (1, 2))
    rnd(0, 1)
    rnd(1, 1)
    gmirror(1, (4, 5))
    gpair(2)
    gmirror(1, (6,))
    loads[6].wait()
    rnd(0, 2)
    g3(1)
    chunk(0)
    rnd(2, 0)
    rnd(1, 2)
    gfar(2)
    gmirror(2, (1, 2, 4, 5))
    rnd(0, 3)
    chunk(1)
    rnd(3, 0)
    rnd(2, 1)
    rnd(1, 3)
    gmirror(2, (6,))
    g3(2)
    turn()
    fin(0)
    rnd(3, 1)
    rnd(2, 2)
    chunk(2)
    rnd(4, 0)
    rnd(3, 2)
    rnd(2, 3)
    fin(1)
    rnd(4, 1)
    last(0)
    last(1)
    rnd(3, 3)
    fin(2)
    rnd(4, 2)
    fin(3)
    rnd(4, 3)
    last(2)
    gdrain()
    mdrain()
    back()
    fin(4)
    last(3)
    last(4)
    rdrain()


def on_device(inputs, out_grad, gate_pre, up_pre, w_down, proj_new, proj_old, first_old, second_old):
    flip = lambda a: jnp.transpose(a, (1, 0, 2))
    shape = jax.ShapeDtypeStruct((3, 16, C), F32)
    dma = pltpu.SemaphoreType.DMA
    low, turned_first, turned_second = pl.pallas_call(
        kernel,
        out_shape=(shape,) * 3,
        in_specs=[pl.BlockSpec(memory_space=pl.ANY)] * 9,
        out_specs=(pl.BlockSpec(memory_space=pl.ANY),) * 3,
        scratch_shapes=[
            pltpu.VMEM((SH, D), BF16),
            pltpu.VMEM((TOK, D), BF16),
            pltpu.VMEM((TOK, 3 * RANK), BF16),
            pltpu.VMEM((D, RANK), BF16),
            pltpu.VMEM((TOK, C), BF16),
            pltpu.VMEM((TOK, C), BF16),
            pltpu.VMEM((C, D), BF16),
            pltpu.VMEM((3, D, RANK), BF16),
            pltpu.VMEM((3, 16, C), F32),
            pltpu.VMEM((3, 16, C), F32),
            pltpu.VMEM((TOK, C), F32),
            pltpu.VMEM((TOK, C), F32),
            pltpu.VMEM((TOK, C), BF16),
            pltpu.VMEM((TOK, CH), F32),
            pltpu.VMEM((TOK, CH), BF16),
            pltpu.VMEM((TOK, CH), BF16),
            pltpu.VMEM((27, RANK, 128), F32),
            pltpu.VMEM((RANK, RANK), F32),
            pltpu.VMEM((2, RANK, RANK), F32),
            pltpu.VMEM((2, RANK, RANK), F32),
            pltpu.VMEM((15, 72, 128), BF16),
            pltpu.VMEM((16, 72, 128), BF16),
            pltpu.VMEM((16, 72, 128), BF16),
            pltpu.VMEM((15, 72, 128), BF16),
            pltpu.VMEM((27, 32, 128), F32),
            pltpu.VMEM((9, 16, C), F32),
            pltpu.VMEM((7, ROWS, 128), BF16),
            pltpu.VMEM((7, ROWS, 128), BF16),
            pltpu.VMEM((XROWS, 128), BF16),
            pltpu.VMEM((XROWS, 128), BF16),
            dma((10,)), dma((3,)), dma((3, 8)), dma, dma, dma, dma,
            dma, dma((NQ, 7)), dma, dma((NQ,)),
        ],
        compiler_params=pltpu.CompilerParams(
            collective_id=0, has_side_effects=True, vmem_limit_bytes=63 * 1024 * 1024
        ),
    )(
        inputs, out_grad, gate_pre, up_pre, w_down, flip(proj_new), flip(proj_old),
        flip(first_old), flip(second_old),
    )
    first = 0.9 * turned_first + 0.1 * low
    second = 0.999 * turned_second + 0.001 * low * low
    return flip(first), flip(second)


def solution(mesh):
    placed = (
        P(("dp", "tensor"), None),
        P(("dp", "tensor"), None),
        P("dp", "tensor"),
        P("dp", "tensor"),
        P("tensor", None),
        P(),
        P("tensor", None, None),
        P("dp", None, "tensor"),
        P("dp", None, "tensor"),
    )
    return jax.shard_map(
        on_device,
        mesh=mesh,
        in_specs=placed,
        out_specs=(P("dp", None, "tensor"), P("dp", None, "tensor")),
        check_vma=False,
    )
```

```python
import jax
import jax.numpy as jnp
from jax import lax
from jax.experimental import pallas as pl
from jax.experimental.pallas import tpu as pltpu
from jax.sharding import PartitionSpec as P

coeff = 0.7978845608028654
F32 = jnp.float32
BF16 = jnp.bfloat16
D = 2304
C = 1152
TOK = 512
SH = 32
RANK = 256
SLAB = 144
CH = 384
QT0 = (0, 5, 9, 15, 21)
QN = (5, 4, 6, 6, 6)
NQ = 5
XF = (False, False, True, False, False)
CR = tuple(16 if f else 32 for f in XF)
XR = tuple(128 if f else 16 for f in XF)
OFF = tuple(sum(QN[i] * CR[i] + 8 for i in range(q)) for q in range(NQ + 1))
XOFF = tuple(sum(QN[i] * XR[i] + 8 for i in range(q)) for q in range(NQ + 1))
ROWS = OFF[NQ]
XROWS = XOFF[NQ]
BACK = (0, 2, 1, 3, 5, 4, 6)
TOP = 181.0
MESH = pl.DeviceIdType.MESH


def top_of(x):
    top = jnp.max(jnp.max(jnp.abs(x), axis=0), axis=0, keepdims=True)
    return jnp.broadcast_to(jnp.maximum(top, 1e-30), (8, 128)).astype(BF16)


def code(x, top):
    n, rows, _ = x.shape
    u = x * (TOP / top.astype(F32))[0:1][None]
    u2 = u * u
    u4 = u2 * u2
    u8 = u4 * u4
    return ((u8 * u4) * (u2 * (u * jnp.abs(u)))).astype(BF16).reshape(n * rows, 128)


def value(v, scale, n):
    v = v.astype(F32)
    r = jnp.exp2(jnp.log2(jnp.abs(v)) * 0.0625)
    return (jnp.where(v < 0.0, -r, r) * (scale * (1.0 / TOP))).reshape(n, -1, 128)


def enc(x, buf):
    n, rows, _ = x.shape
    top = top_of(x)
    buf[pl.ds(n * rows, 8)] = top
    buf[pl.ds(0, n * rows)] = code(x, top)


def dec(buf, n, rows):
    scale = buf[pl.ds(n * rows, 8)].astype(F32)[0:1]
    return value(buf[pl.ds(0, n * rows)], scale, n)


def enc2(a, b, buf):
    ta, tb = top_of(a), top_of(b)
    first = lax.broadcasted_iota(jnp.int32, (8, 128), 0) < 4
    buf[pl.ds(64, 8)] = jnp.where(first, ta.astype(F32), tb.astype(F32)).astype(BF16)
    buf[pl.ds(0, 32)] = code(a, ta)
    buf[pl.ds(32, 32)] = code(b, tb)


def dec2(buf):
    scale = buf[pl.ds(64, 8)].astype(F32)
    return value(buf[pl.ds(0, 32)], scale[0:1], 2), value(buf[pl.ds(32, 32)], scale[4:5], 2)


def kernel(
    inp_h, og_h, gate_h, up_h, w_h, pn_h, po_h, fo_h, so_h,
    low_h, tf_h, ts_h,
    inp, Y, Pb, po, gate, up, w, pn, fo, so, V, U, G, H, GG, UG, L, R, M, T, MS, MR, TS, TB, FIN, OUT, RA, RB, RC, RD,
    rsend, rrecv, xsend, xrecv,
    ld, gs, gr, ms, mr, ts, tr, rs, rr, xs, xr, ras, rar, rcs, rcr,
):
    d = lax.axis_index("dp")
    t = lax.axis_index("tensor")
    z = d // 2
    xh = lax.rem(d, 2)
    c = lax.rem(t, 2)
    y = lax.rem(t // 2, 4)
    xl = t // 8
    kd = jnp.minimum(d // 5, 2)

    def tid(a, b):
        return a * 8 + b * 2 + c

    yn = lax.rem(y + 1, 4)
    yb = lax.rem(y + 3, 4)
    y2 = lax.rem(y + 2, 4)
    xo = 1 - xl
    sib = t + 1 - 2 * c
    xp = tid(xo, y)
    yp = tid(xl, yn)
    ym = tid(xl, yb)
    zn = lax.rem(z + 1, 8)
    zb = lax.rem(z + 7, 8)
    zlong = jnp.where(c == 0, zn, zb)
    zshort = jnp.where(c == 0, zb, zn)
    dlong = zlong * 2 + xh
    dshort = zshort * 2 + xh
    dx = d + 1 - 2 * xh
    step = 1 - 2 * c

    def loc(src, dst, i):
        return pltpu.make_async_copy(src, dst, ld.at[i])

    own = pl.ds(pl.multiple_of(t * SH, SH), SH)
    loads = [
        loc(og_h, Y.at[own], 0),
        loc(inp_h, inp, 1),
        loc(pn_h.at[2], pn.at[2], 2),
        loc(po_h.at[kd], po, 3),
        loc(gate_h, gate, 4),
        loc(up_h, up, 5),
        loc(w_h, w, 6),
        loc(fo_h, fo, 7),
        loc(so_h, so, 8),
        loc(pn_h.at[0], pn.at[0], 10),
        loc(pn_h.at[1], pn.at[1], 11),
    ]
    for i in (0, 2, 1, 9, 10, 7, 8, 3):
        loads[i].start()

    bar = pltpu.get_barrier_semaphore()
    lane = (xp, yp, ym, tid(xl, y2), tid(xo, yn), tid(xo, yb), tid(xo, y2))

    @pl.loop(1, 16)
    def _(j):
        pl.semaphore_signal(
            bar, inc=1, device_id={"tensor": lax.rem(t + j, 16)}, device_id_type=MESH
        )
        pl.semaphore_signal(
            bar, inc=1, device_id={"dp": lax.rem(d + j, 16)}, device_id_type=MESH
        )

    pay = ((Pb, SH, SH), (Y, SH, SH))

    def gcopy(p, slot, target, i):
        buf, rows, mult = pay[p]
        sl = pl.ds(pl.multiple_of(slot * rows, mult), rows)
        return pltpu.make_async_remote_copy(
            src_ref=buf.at[sl], dst_ref=buf.at[sl], send_sem=gs.at[p],
            recv_sem=gr.at[p, i], device_id={"tensor": target}, device_id_type=MESH,
        )

    def gsend(p, slot, target, i):
        gcopy(p, slot, target, i).start()

    def gwait(p, j):
        gcopy(p, lane[j], sib, j).wait_recv()

    def shards(p, n, sem):
        buf, rows, _ = pay[p]
        part = buf.at[pl.ds(0, n * rows)]
        pltpu.make_async_copy(part, part, sem).wait()

    def project():
        for a in (0, 2, 1, 9, 10):
            loads[a].wait()
            if a in (0, 1):
                continue
            k = (2, 0, 1)[(2, 9, 10).index(a)]
            lhs = inp[...] if k < 2 else Y[own, :]
            Pb[own, k * RANK : (k + 1) * RANK] = jnp.dot(
                lhs, pn[k], preferred_element_type=F32
            ).astype(BF16)
        for i in (4, 5, 6):
            loads[i].start()

    def gown(p, n):
        for j in range(n):
            gsend(p, t, lane[j], BACK[j])
        gsend(p, t, sib, 7)

    def gmirror(p, js):
        for j in js:
            gwait(p, j)
            gsend(p, lane[j], sib, 7 if j in (1, 2, 3) else 8)

    def gpair(p):
        gwait(p, 0)
        gsend(p, xp, yp, 5)
        gsend(p, xp, ym, 4)
        gsend(p, xp, sib, 8)

    def gfar(p):
        gwait(p, 3)
        gsend(p, lane[3], xp, 6)
        gsend(p, lane[3], sib, 7)

    def g3(p, side):
        shards(p, 4, gr.at[p, 7 + side])

    def rpart():
        loads[3].wait()
        slab = pl.ds(pl.multiple_of(t * SLAB, 16), SLAB)
        R[...] = lax.dot_general(
            pn[kd, slab, :], po[...], (((0,), (0,)), ((), ())), preferred_element_type=F32
        )
        for j in range(16):
            rows = slice(16 * j, 16 * j + 16)
            enc(jnp.stack([R[rows, 0:128], R[rows, 128:256]]), RA.at[j])

    def spread(src, dst, ssem, rsem):
        @pl.loop(1, 16)
        def _(i):
            j = lax.rem(t + i, 16)
            pltpu.make_async_remote_copy(
                src_ref=src(j), dst_ref=dst, send_sem=ssem, recv_sem=rsem,
                device_id={"tensor": j}, device_id_type=MESH,
            ).start()

        pltpu.make_async_copy(src(t), dst, rsem).start()

    def rsend1():
        spread(lambda j: RA.at[j], RB.at[t], ras, rar)

    def rsum():
        pltpu.make_async_copy(RB, RB, rar).wait()
        x = dec(RB.at[0], 2, 16)
        for j in range(1, 16):
            x = x + dec(RB.at[j], 2, 16)
        enc(x, RC)
        spread(lambda j: RC, RD.at[t], rcs, rcr)

    def mrem(o):
        return pltpu.make_async_remote_copy(
            src_ref=MS.at[o], dst_ref=MR.at[d], send_sem=ms, recv_sem=mr,
            device_id={"dp": o}, device_id_type=MESH,
        )

    def menc():
        loads[7].wait()
        loads[8].wait()
        for o in range(15):
            c0 = min((o % 5) * 256, 896)
            pair = [
                jnp.stack([ref[o // 5, :, c0 + i * 128 : c0 + i * 128 + 128] for i in range(2)])
                for ref in (fo, so)
            ]
            enc2(*pair, MS.at[o])

    def msend(par):
        @pl.loop(0, 8)
        def _(j):
            o = 2 * j + par

            @pl.when(jnp.logical_and(o < 15, o != d))
            def _():
                mrem(o).start()

            @pl.when(jnp.logical_and(o < 15, o == d))
            def _():
                pltpu.make_async_copy(MS.at[o], MR.at[d], mr).start()

    def trem(dst):
        return pltpu.make_async_remote_copy(
            src_ref=TS.at[dst], dst_ref=TB.at[d], send_sem=ts, recv_sem=tr,
            device_id={"dp": dst}, device_id_type=MESH,
        )

    def turn():
        pltpu.make_async_copy(RD, RD, rcr).wait()

        @pl.when(d < 15)
        def _():
            pltpu.make_async_copy(MR, MR, mr).wait()

            @pl.loop(0, 16)
            def _(s):
                rows = pl.ds(pl.multiple_of(s * 16, 16), 16)
                for m, x in enumerate(dec2(MR.at[s])):
                    M[m, rows, 0:128] = x[0]
                    M[m, rows, 128:256] = x[1]

            for j in range(16):
                x = dec(RD.at[j], 2, 16)
                R[16 * j : 16 * j + 16, 0:128] = x[0]
                R[16 * j : 16 * j + 16, 128:256] = x[1]
            rot = R[...]
            for m in range(2):
                T[m] = jnp.dot(
                    rot if m == 0 else rot * rot, M[m],
                    precision=lax.Precision.HIGHEST, preferred_element_type=F32,
                )

    def tsend(lo, hi):
        @pl.when(d < 15)
        def _():
            @pl.loop(lo, hi)
            def _(i):
                j = lax.rem(d + i, 16)
                rows = pl.ds(pl.multiple_of(j * 16, 16), 16)
                pair = [jnp.stack([T[m, rows, 0:128], T[m, rows, 128:256]]) for m in range(2)]
                enc2(*pair, TS.at[j])

                @pl.when(i > 0)
                def _():
                    trem(j).start()

                @pl.when(i == 0)
                def _():
                    pltpu.make_async_copy(TS.at[j], TB.at[d], tr).start()

    def span(q):
        return pl.ds(OFF[q], OFF[q + 1] - OFF[q])

    def xspan(q):
        return pl.ds(XOFF[q], XOFF[q + 1] - XOFF[q])

    def rcopy(q, i):
        sp = span(q)
        return pltpu.make_async_remote_copy(
            src_ref=rsend.at[i, sp], dst_ref=rrecv.at[i, sp], send_sem=rs, recv_sem=rr.at[q, i],
            device_id={"dp": dlong if i < 4 else dshort}, device_id_type=MESH,
        )

    def mine(q, zdest):
        tiles = pl.ds(QT0[q], QN[q])
        if XF[q]:
            return L[tiles, zdest, xh]
        return L[tiles, zdest].reshape(QN[q], 32, 128)

    def rnd(q, r):
        n = QN[q]
        tiles = span(q)
        for i, far in ((r, step * (4 - r)), (4 + r, -step * (3 - r))):
            if i == 7:
                continue
            x = mine(q, lax.rem(z + 8 + far, 8))
            if r > 0:
                rcopy(q, i - 1).wait_recv()
                x = x + dec(rrecv.at[i - 1, tiles], n, CR[q])
            enc(x, rsend.at[i, tiles])
            rcopy(q, i).start()

    def xcopy(q):
        sp = xspan(q)
        return pltpu.make_async_remote_copy(
            src_ref=xsend.at[sp], dst_ref=xrecv.at[sp], send_sem=xs, recv_sem=xr.at[q],
            device_id={"dp": dx}, device_id_type=MESH,
        )

    def xout(q):
        n = QN[q]
        x = L[pl.ds(QT0[q], n), :, 1 - xh]
        enc(x.reshape(n, 128, 128), xsend.at[xspan(q)])
        xcopy(q).start()

    def xin(q):
        n = QN[q]
        tiles = pl.ds(QT0[q], n)
        xcopy(q).wait_recv()
        x = dec(xrecv.at[xspan(q)], n, 128)
        L[tiles, :, xh] = L[tiles, :, xh] + x.reshape(n, 8, 16, 128)

    def emit(q, low):
        n = QN[q]
        for i in range(n):
            g = QT0[q] + i
            k, ct = (2, g) if g < 9 else ((g - 9) % 6 // 3, (g - 9) // 6 * 3 + (g - 9) % 3)
            OUT[k, :, ct * 128 : (ct + 1) * 128] = low[i]
        if q < 2:
            part = (2, slice(None), pl.ds(QT0[q] * 128, n * 128))
        else:
            part = (pl.ds(0, 2), slice(None), pl.ds((q - 2) * CH, CH))
        pltpu.make_async_copy(OUT.at[part], low_h.at[part], ld.at[9]).start()

    def fin(q):
        n = QN[q]
        tiles = span(q)
        dst = pl.ds(QT0[q], n)
        rcopy(q, 3).wait_recv()
        rcopy(q, 6).wait_recv()
        x = mine(q, z) + dec(rrecv.at[3, tiles], n, CR[q]) + dec(rrecv.at[6, tiles], n, CR[q])
        if XF[q]:
            emit(q, x)
            return
        FIN[dst] = x
        enc(FIN[dst, pl.ds(pl.multiple_of((1 - xh) * 16, 16), 16), :], xsend.at[xspan(q)])
        xcopy(q).start()

    def last(q):
        n = QN[q]
        dst = pl.ds(QT0[q], n)
        xcopy(q).wait_recv()
        emit(
            q,
            FIN[dst, pl.ds(pl.multiple_of(xh * 16, 16), 16), :]
            + dec(xrecv.at[xspan(q)], n, 16),
        )

    def back():
        pltpu.make_async_copy(TB, TB, tr).wait()
        for o in range(15):
            for m, x in enumerate(dec2(TB.at[o])):
                for i in range(2):
                    ct = min(2 * (o % 5), 7) + i
                    if o % 5 < 4 or i == 1:
                        OUT[3 + 3 * m + o // 5, :, ct * 128 : (ct + 1) * 128] = x[i]
        loc(OUT.at[pl.ds(3, 3)], tf_h, 9).start()
        loc(OUT.at[pl.ds(6, 3)], ts_h, 9).start()

    project()
    pl.semaphore_wait(bar, 30)
    gown(0, 7)
    gown(1, 4)
    menc()
    msend(xh)
    rpart()
    loads[4].wait()
    loads[5].wait()

    def act(lo, hi):
        @pl.loop(lo, hi)
        def _(i):
            rows = pl.ds(pl.multiple_of(i * 16, 16), 16)
            g = gate[rows, :].astype(F32)
            u = up[rows, :].astype(F32)
            g2_ = g * g
            tv = jnp.tanh(coeff * (g + 0.044715 * (g2_ * g)))
            val = 0.5 * g * (1.0 + tv)
            slope = 0.5 * (1.0 + tv) + 0.5 * g * (1.0 - tv * tv) * (
                coeff * (1.0 + 3.0 * 0.044715 * g2_)
            )
            V[rows, :] = val
            U[rows, :] = u * slope
            G[rows, :] = (val * u).astype(BF16)

    contract = (((0,), (0,)), ((), ()))

    def lowd():
        for j in range(3):
            r = lax.dot_general(
                Pb[:, 2 * RANK : 3 * RANK], G[:, j * CH : (j + 1) * CH], contract,
                preferred_element_type=F32,
            )
            for i in range(3):
                L[3 * j + i] = r[:, i * 128 : (i + 1) * 128].reshape(8, 2, 16, 128)

    def chunk(j, side):
        cols = slice(j * CH, (j + 1) * CH)
        row0 = (xl if side == 0 else xo) * 256
        part = pl.ds(pl.multiple_of(row0, 256), 256)
        H[...] = lax.dot_general(
            Y[part, :], w[cols, :], (((1,), (1,)), ((), ())), preferred_element_type=F32
        )

        @pl.loop(0, 8)
        def _(i):
            rows = pl.ds(pl.multiple_of(i * 32, 32), 32)
            from_ = pl.ds(pl.multiple_of(row0 + i * 32, 32), 32)
            h = H[rows, :]
            GG[rows, :] = (h * U[from_, cols]).astype(BF16)
            UG[rows, :] = (h * V[from_, cols]).astype(BF16)

        for k, ref in enumerate((GG, UG)):
            r = lax.dot_general(
                Pb[part, k * RANK : (k + 1) * RANK], ref[...], contract,
                preferred_element_type=F32,
            )
            for i in range(3):
                tile = r[:, i * 128 : (i + 1) * 128].reshape(8, 2, 16, 128)
                g = 9 + 6 * j + 3 * k + i
                L[g] = tile if side == 0 else L[g] + tile

    def gdrain():
        for p in range(2):
            shards(p, 15, gs.at[p])
        part = RA.at[pl.ds(0, 15)]
        pltpu.make_async_copy(part, part, ras).wait()
        pltpu.make_async_copy(part, part, rcs).wait()

    def mdrain():
        @pl.when(d < 15)
        def _():
            part = MS.at[pl.ds(0, 14)]
            pltpu.make_async_copy(part, part, ms).wait()
            part = TS.at[pl.ds(0, 15)]
            pltpu.make_async_copy(part, part, ts).wait()

        @pl.when(d == 15)
        def _():
            pltpu.make_async_copy(MS, MS, ms).wait()

    def rdrain():
        pltpu.make_async_copy(rsend, rsend, rs).wait()
        pltpu.make_async_copy(xsend, xsend, xs).wait()
        pltpu.make_async_copy(OUT, OUT, ld.at[9]).wait()

    act(0, 32)
    gmirror(0, range(7))
    g3(0, 0)
    g3(0, 1)
    lowd()
    rnd(0, 0)
    rnd(1, 0)
    gpair(1)
    rsend1()
    gmirror(1, (1, 2))
    gfar(1)
    msend(1 - xh)
    rnd(0, 1)
    rnd(1, 1)
    loads[6].wait()
    g3(1, 0)
    chunk(0, 0)
    gmirror(1, (4, 5))
    chunk(1, 0)
    rsum()
    gmirror(1, (6,))
    chunk(2, 0)
    g3(1, 1)
    chunk(0, 1)
    xout(2)
    rnd(0, 2)
    rnd(1, 2)
    chunk(1, 1)
    rnd(3, 0)
    chunk(2, 1)
    rnd(4, 0)
    rnd(0, 3)
    rnd(1, 3)
    turn()
    tsend(0, 4)
    rnd(3, 1)
    xin(2)
    rnd(2, 0)
    rnd(4, 1)
    tsend(4, 8)
    rnd(3, 2)
    rnd(2, 1)
    rnd(4, 2)
    tsend(8, 12)
    fin(0)
    fin(1)
    rnd(3, 3)
    rnd(2, 2)
    tsend(12, 16)
    rnd(4, 3)
    fin(3)
    rnd(2, 3)
    gdrain()
    mdrain()
    last(0)
    last(1)
    fin(4)
    last(3)
    fin(2)
    back()
    last(4)
    rdrain()


def on_device(inputs, out_grad, gate_pre, up_pre, w_down, proj_new, proj_old, first_old, second_old):
    flip = lambda a: jnp.transpose(a, (1, 0, 2))
    shape = jax.ShapeDtypeStruct((3, 16, C), F32)
    dma = pltpu.SemaphoreType.DMA
    low, turned_first, turned_second = pl.pallas_call(
        kernel,
        out_shape=(shape,) * 3,
        in_specs=[pl.BlockSpec(memory_space=pl.ANY)] * 9,
        out_specs=(pl.BlockSpec(memory_space=pl.ANY),) * 3,
        scratch_shapes=[
            pltpu.VMEM((SH, D), BF16),
            pltpu.VMEM((TOK, D), BF16),
            pltpu.VMEM((TOK, 3 * RANK), BF16),
            pltpu.VMEM((SLAB, RANK), BF16),
            pltpu.VMEM((TOK, C), BF16),
            pltpu.VMEM((TOK, C), BF16),
            pltpu.VMEM((C, D), BF16),
            pltpu.VMEM((3, D, RANK), BF16),
            pltpu.VMEM((3, 16, C), F32),
            pltpu.VMEM((3, 16, C), F32),
            pltpu.VMEM((TOK, C), F32),
            pltpu.VMEM((TOK, C), F32),
            pltpu.VMEM((TOK, C), BF16),
            pltpu.VMEM((256, CH), F32),
            pltpu.VMEM((256, CH), BF16),
            pltpu.VMEM((256, CH), BF16),
            pltpu.VMEM((27, 8, 2, 16, 128), F32),
            pltpu.VMEM((RANK, RANK), F32),
            pltpu.VMEM((2, RANK, RANK), F32),
            pltpu.VMEM((2, RANK, RANK), F32),
            pltpu.VMEM((15, 72, 128), BF16),
            pltpu.VMEM((16, 72, 128), BF16),
            pltpu.VMEM((16, 72, 128), BF16),
            pltpu.VMEM((15, 72, 128), BF16),
            pltpu.VMEM((27, 32, 128), F32),
            pltpu.VMEM((9, 16, C), F32),
            pltpu.VMEM((16, 40, 128), BF16),
            pltpu.VMEM((16, 40, 128), BF16),
            pltpu.VMEM((40, 128), BF16),
            pltpu.VMEM((16, 40, 128), BF16),
            pltpu.VMEM((7, ROWS, 128), BF16),
            pltpu.VMEM((7, ROWS, 128), BF16),
            pltpu.VMEM((XROWS, 128), BF16),
            pltpu.VMEM((XROWS, 128), BF16),
            dma((12,)), dma((2,)), dma((2, 9)), dma, dma, dma, dma,
            dma, dma((NQ, 7)), dma, dma((NQ,)), dma, dma, dma, dma,
        ],
        compiler_params=pltpu.CompilerParams(
            collective_id=0, has_side_effects=True, vmem_limit_bytes=63 * 1024 * 1024
        ),
    )(
        inputs, out_grad, gate_pre, up_pre, w_down, flip(proj_new), flip(proj_old),
        flip(first_old), flip(second_old),
    )
    first = 0.9 * turned_first + 0.1 * low
    second = 0.999 * turned_second + 0.001 * low * low
    return flip(first), flip(second)


def solution(mesh):
    placed = (
        P(("dp", "tensor"), None),
        P(("dp", "tensor"), None),
        P("dp", "tensor"),
        P("dp", "tensor"),
        P("tensor", None),
        P(),
        P("tensor", None, None),
        P("dp", None, "tensor"),
        P("dp", None, "tensor"),
    )
    return jax.shard_map(
        on_device,
        mesh=mesh,
        in_specs=placed,
        out_specs=(P("dp", None, "tensor"), P("dp", None, "tensor")),
        check_vma=False,
    )
```

```python
import jax
import jax.numpy as jnp
from jax import lax
from jax.experimental import pallas as pl
from jax.experimental.pallas import tpu as pltpu
from jax.sharding import PartitionSpec as P

coeff = 0.7978845608028654
F32 = jnp.float32
BF16 = jnp.bfloat16
D = 2304
C = 1152
TOK = 512
SH = 32
RANK = 256
SLAB = 144
CH = 384
QT0 = (0, 5, 9, 15, 21)
QN = (5, 4, 6, 6, 6)
NQ = 5
XF = (False, False, True, False, False)
CR = tuple(16 if f else 32 for f in XF)
XR = tuple(128 if f else 16 for f in XF)
OFF = tuple(sum(QN[i] * CR[i] + 8 for i in range(q)) for q in range(NQ + 1))
XOFF = tuple(sum(QN[i] * XR[i] + 8 for i in range(q)) for q in range(NQ + 1))
ROWS = OFF[NQ]
XROWS = XOFF[NQ]
BACK = (0, 2, 1, 3, 5, 4, 6)
TOP = 181.0
MESH = pl.DeviceIdType.MESH


def top_of(x):
    top = jnp.max(jnp.max(jnp.abs(x), axis=0), axis=0, keepdims=True)
    return jnp.broadcast_to(jnp.maximum(top, 1e-30), (8, 128)).astype(BF16)


def code(x, top):
    n, rows, _ = x.shape
    u = x * (TOP / top.astype(F32))[0:1][None]
    u2 = u * u
    u4 = u2 * u2
    u8 = u4 * u4
    return ((u8 * u4) * (u2 * (u * jnp.abs(u)))).astype(BF16).reshape(n * rows, 128)


def value(v, scale, n):
    v = v.astype(F32)
    r = jnp.exp2(jnp.log2(jnp.abs(v)) * 0.0625)
    return (jnp.where(v < 0.0, -r, r) * (scale * (1.0 / TOP))).reshape(n, -1, 128)


def enc(x, buf):
    n, rows, _ = x.shape
    top = top_of(x)
    buf[pl.ds(n * rows, 8)] = top
    buf[pl.ds(0, n * rows)] = code(x, top)


def dec(buf, n, rows):
    scale = buf[pl.ds(n * rows, 8)].astype(F32)[0:1]
    return value(buf[pl.ds(0, n * rows)], scale, n)


def enc2(a, b, buf):
    ta, tb = top_of(a), top_of(b)
    first = lax.broadcasted_iota(jnp.int32, (8, 128), 0) < 4
    buf[pl.ds(64, 8)] = jnp.where(first, ta.astype(F32), tb.astype(F32)).astype(BF16)
    buf[pl.ds(0, 32)] = code(a, ta)
    buf[pl.ds(32, 32)] = code(b, tb)


def dec2(buf):
    scale = buf[pl.ds(64, 8)].astype(F32)
    return value(buf[pl.ds(0, 32)], scale[0:1], 2), value(buf[pl.ds(32, 32)], scale[4:5], 2)


def kernel(
    inp_h, og_h, gate_h, up_h, w_h, pn_h, po_h, fo_h, so_h,
    low_h, tf_h, ts_h,
    inp, Y, Pb, po, gate, up, w, pn, fo, so, V, U, G, H, GG, UG, L, R, M, T, MS, MR, TS, TB, FIN, OUT, RA, RB, RC, RD,
    rsend, rrecv, xsend, xrecv,
    ld, gs, gr, ms, mr, ts, tr, rs, rr, xs, xr, ras, rar, rcs, rcr,
):
    d = lax.axis_index("dp")
    t = lax.axis_index("tensor")
    z = d // 2
    xh = lax.rem(d, 2)
    c = lax.rem(t, 2)
    y = lax.rem(t // 2, 4)
    xl = t // 8
    kd = jnp.minimum(d // 5, 2)

    def tid(a, b):
        return a * 8 + b * 2 + c

    yn = lax.rem(y + 1, 4)
    yb = lax.rem(y + 3, 4)
    y2 = lax.rem(y + 2, 4)
    xo = 1 - xl
    sib = t + 1 - 2 * c
    xp = tid(xo, y)
    yp = tid(xl, yn)
    ym = tid(xl, yb)
    zn = lax.rem(z + 1, 8)
    zb = lax.rem(z + 7, 8)
    zlong = jnp.where(c == 0, zn, zb)
    zshort = jnp.where(c == 0, zb, zn)
    dlong = zlong * 2 + xh
    dshort = zshort * 2 + xh
    dfar = lax.rem(z + 8 + 2 * (1 - 2 * c), 8) * 2 + xh
    dx = d + 1 - 2 * xh
    step = 1 - 2 * c

    def loc(src, dst, i):
        return pltpu.make_async_copy(src, dst, ld.at[i])

    own = pl.ds(pl.multiple_of(t * SH, SH), SH)
    loads = [
        loc(og_h, Y.at[own], 0),
        loc(inp_h, inp, 1),
        loc(pn_h.at[2], pn.at[2], 2),
        loc(po_h.at[kd], po, 3),
        loc(gate_h, gate, 4),
        loc(up_h, up, 5),
        loc(w_h, w, 6),
        loc(fo_h, fo, 7),
        loc(so_h, so, 8),
        loc(pn_h.at[0], pn.at[0], 10),
        loc(pn_h.at[1], pn.at[1], 11),
    ]
    for i in (0, 2, 1, 9, 10, 7, 8, 3):
        loads[i].start()

    bar = pltpu.get_barrier_semaphore()
    lane = (xp, yp, ym, tid(xl, y2), tid(xo, yn), tid(xo, yb), tid(xo, y2))

    @pl.loop(1, 16)
    def _(j):
        pl.semaphore_signal(
            bar, inc=1, device_id={"tensor": lax.rem(t + j, 16)}, device_id_type=MESH
        )
        pl.semaphore_signal(
            bar, inc=1, device_id={"dp": lax.rem(d + j, 16)}, device_id_type=MESH
        )

    pay = ((Pb, SH, SH), (Y, SH, SH))

    def gcopy(p, slot, target, i):
        buf, rows, mult = pay[p]
        sl = pl.ds(pl.multiple_of(slot * rows, mult), rows)
        return pltpu.make_async_remote_copy(
            src_ref=buf.at[sl], dst_ref=buf.at[sl], send_sem=gs.at[p],
            recv_sem=gr.at[p, i], device_id={"tensor": target}, device_id_type=MESH,
        )

    def gsend(p, slot, target, i):
        gcopy(p, slot, target, i).start()

    def gwait(p, j):
        gcopy(p, lane[j], sib, j).wait_recv()

    def shards(p, n, sem):
        buf, rows, _ = pay[p]
        part = buf.at[pl.ds(0, n * rows)]
        pltpu.make_async_copy(part, part, sem).wait()

    def project():
        for a in (0, 2, 1, 9, 10):
            loads[a].wait()
            if a in (0, 1):
                continue
            k = (2, 0, 1)[(2, 9, 10).index(a)]
            lhs = inp[...] if k < 2 else Y[own, :]
            Pb[own, k * RANK : (k + 1) * RANK] = jnp.dot(
                lhs, pn[k], preferred_element_type=F32
            ).astype(BF16)
        for i in (4, 5, 6):
            loads[i].start()

    def gown(p, n):
        for j in range(n):
            gsend(p, t, lane[j], BACK[j])
        gsend(p, t, sib, 7)

    def gmirror(p, js):
        for j in js:
            gwait(p, j)
            gsend(p, lane[j], sib, 7 if j in (1, 2, 3) else 8)

    def gpair(p):
        gwait(p, 0)
        gsend(p, xp, yp, 5)
        gsend(p, xp, ym, 4)
        gsend(p, xp, sib, 8)

    def gfar(p):
        gwait(p, 3)
        gsend(p, lane[3], xp, 6)
        gsend(p, lane[3], sib, 7)

    def g3(p, side):
        shards(p, 4, gr.at[p, 7 + side])

    def rpart():
        loads[3].wait()
        slab = pl.ds(pl.multiple_of(t * SLAB, 16), SLAB)
        R[...] = lax.dot_general(
            pn[kd, slab, :], po[...], (((0,), (0,)), ((), ())), preferred_element_type=F32
        )
        for j in range(16):
            rows = slice(16 * j, 16 * j + 16)
            enc(jnp.stack([R[rows, 0:128], R[rows, 128:256]]), RA.at[j])

    def spread(src, dst, ssem, rsem):
        @pl.loop(1, 16)
        def _(i):
            j = lax.rem(t + i, 16)
            pltpu.make_async_remote_copy(
                src_ref=src(j), dst_ref=dst, send_sem=ssem, recv_sem=rsem,
                device_id={"tensor": j}, device_id_type=MESH,
            ).start()

        pltpu.make_async_copy(src(t), dst, rsem).start()

    def rsend1():
        spread(lambda j: RA.at[j], RB.at[t], ras, rar)

    def rsum():
        pltpu.make_async_copy(RB, RB, rar).wait()
        x = dec(RB.at[0], 2, 16)
        for j in range(1, 16):
            x = x + dec(RB.at[j], 2, 16)
        enc(x, RC)
        spread(lambda j: RC, RD.at[t], rcs, rcr)

    def mrem(o):
        return pltpu.make_async_remote_copy(
            src_ref=MS.at[o], dst_ref=MR.at[d], send_sem=ms, recv_sem=mr,
            device_id={"dp": o}, device_id_type=MESH,
        )

    def menc():
        loads[7].wait()
        loads[8].wait()
        for o in range(15):
            c0 = min((o % 5) * 256, 896)
            pair = [
                jnp.stack([ref[o // 5, :, c0 + i * 128 : c0 + i * 128 + 128] for i in range(2)])
                for ref in (fo, so)
            ]
            enc2(*pair, MS.at[o])

    def msend(par):
        @pl.loop(0, 8)
        def _(j):
            o = 2 * j + par

            @pl.when(jnp.logical_and(o < 15, o != d))
            def _():
                mrem(o).start()

            @pl.when(jnp.logical_and(o < 15, o == d))
            def _():
                pltpu.make_async_copy(MS.at[o], MR.at[d], mr).start()

    def trem(dst):
        return pltpu.make_async_remote_copy(
            src_ref=TS.at[dst], dst_ref=TB.at[d], send_sem=ts, recv_sem=tr,
            device_id={"dp": dst}, device_id_type=MESH,
        )

    def turn():
        pltpu.make_async_copy(RD, RD, rcr).wait()

        @pl.when(d < 15)
        def _():
            pltpu.make_async_copy(MR, MR, mr).wait()

            @pl.loop(0, 16)
            def _(s):
                rows = pl.ds(pl.multiple_of(s * 16, 16), 16)
                for m, x in enumerate(dec2(MR.at[s])):
                    M[m, rows, 0:128] = x[0]
                    M[m, rows, 128:256] = x[1]

            for j in range(16):
                x = dec(RD.at[j], 2, 16)
                R[16 * j : 16 * j + 16, 0:128] = x[0]
                R[16 * j : 16 * j + 16, 128:256] = x[1]
            rot = R[...]
            for m in range(2):
                T[m] = jnp.dot(
                    rot if m == 0 else rot * rot, M[m],
                    precision=lax.Precision.HIGHEST, preferred_element_type=F32,
                )

    def tsend(lo, hi):
        @pl.when(d < 15)
        def _():
            @pl.loop(lo, hi)
            def _(i):
                j = lax.rem(d + i, 16)
                rows = pl.ds(pl.multiple_of(j * 16, 16), 16)
                pair = [jnp.stack([T[m, rows, 0:128], T[m, rows, 128:256]]) for m in range(2)]
                enc2(*pair, TS.at[j])

                @pl.when(i > 0)
                def _():
                    trem(j).start()

                @pl.when(i == 0)
                def _():
                    pltpu.make_async_copy(TS.at[j], TB.at[d], tr).start()

    def span(q):
        return pl.ds(OFF[q], OFF[q + 1] - OFF[q])

    def xspan(q):
        return pl.ds(XOFF[q], XOFF[q + 1] - XOFF[q])

    def rcopy(q, i):
        sp = span(q)
        return pltpu.make_async_remote_copy(
            src_ref=rsend.at[i, sp], dst_ref=rrecv.at[i, sp], send_sem=rs, recv_sem=rr.at[q, i],
            device_id={"dp": dlong if i < 3 else dshort if i < 6 else dfar}, device_id_type=MESH,
        )

    def mine(q, zdest):
        tiles = pl.ds(QT0[q], QN[q])
        if XF[q]:
            return L[tiles, zdest, xh]
        return L[tiles, zdest].reshape(QN[q], 32, 128)

    def rnd(q, r):
        n = QN[q]
        tiles = span(q)
        for i, far in ((6, 4), (r, step * (3 - r)), (3 + r, -step * (3 - r))):
            if i == 6 and r > 0:
                continue
            x = mine(q, lax.rem(z + 8 + far, 8))
            if r > 0:
                rcopy(q, i - 1).wait_recv()
                x = x + dec(rrecv.at[i - 1, tiles], n, CR[q])
            if i == 1:
                rcopy(q, 6).wait_recv()
                x = x + dec(rrecv.at[6, tiles], n, CR[q])
            enc(x, rsend.at[i, tiles])
            rcopy(q, i).start()

    def xcopy(q):
        sp = xspan(q)
        return pltpu.make_async_remote_copy(
            src_ref=xsend.at[sp], dst_ref=xrecv.at[sp], send_sem=xs, recv_sem=xr.at[q],
            device_id={"dp": dx}, device_id_type=MESH,
        )

    def xout(q):
        n = QN[q]
        x = L[pl.ds(QT0[q], n), :, 1 - xh]
        enc(x.reshape(n, 128, 128), xsend.at[xspan(q)])
        xcopy(q).start()

    def xin(q):
        n = QN[q]
        tiles = pl.ds(QT0[q], n)
        xcopy(q).wait_recv()
        x = dec(xrecv.at[xspan(q)], n, 128)
        L[tiles, :, xh] = L[tiles, :, xh] + x.reshape(n, 8, 16, 128)

    def emit(q, low):
        n = QN[q]
        for i in range(n):
            g = QT0[q] + i
            k, ct = (2, g) if g < 9 else ((g - 9) % 6 // 3, (g - 9) // 6 * 3 + (g - 9) % 3)
            OUT[k, :, ct * 128 : (ct + 1) * 128] = low[i]
        if q < 2:
            part = (2, slice(None), pl.ds(QT0[q] * 128, n * 128))
        else:
            part = (pl.ds(0, 2), slice(None), pl.ds((q - 2) * CH, CH))
        pltpu.make_async_copy(OUT.at[part], low_h.at[part], ld.at[9]).start()

    def fin(q):
        n = QN[q]
        tiles = span(q)
        dst = pl.ds(QT0[q], n)
        rcopy(q, 2).wait_recv()
        rcopy(q, 5).wait_recv()
        x = mine(q, z) + dec(rrecv.at[2, tiles], n, CR[q]) + dec(rrecv.at[5, tiles], n, CR[q])
        if XF[q]:
            emit(q, x)
            return
        FIN[dst] = x
        enc(FIN[dst, pl.ds(pl.multiple_of((1 - xh) * 16, 16), 16), :], xsend.at[xspan(q)])
        xcopy(q).start()

    def last(q):
        n = QN[q]
        dst = pl.ds(QT0[q], n)
        xcopy(q).wait_recv()
        emit(
            q,
            FIN[dst, pl.ds(pl.multiple_of(xh * 16, 16), 16), :]
            + dec(xrecv.at[xspan(q)], n, 16),
        )

    def back():
        pltpu.make_async_copy(TB, TB, tr).wait()
        for o in range(15):
            for m, x in enumerate(dec2(TB.at[o])):
                for i in range(2):
                    ct = min(2 * (o % 5), 7) + i
                    if o % 5 < 4 or i == 1:
                        OUT[3 + 3 * m + o // 5, :, ct * 128 : (ct + 1) * 128] = x[i]
        loc(OUT.at[pl.ds(3, 3)], tf_h, 9).start()
        loc(OUT.at[pl.ds(6, 3)], ts_h, 9).start()

    project()
    pl.semaphore_wait(bar, 30)
    gown(0, 7)
    gown(1, 4)
    menc()
    msend(xh)
    rpart()
    loads[4].wait()
    loads[5].wait()

    def act(lo, hi):
        @pl.loop(lo, hi)
        def _(i):
            rows = pl.ds(pl.multiple_of(i * 16, 16), 16)
            g = gate[rows, :].astype(F32)
            u = up[rows, :].astype(F32)
            g2_ = g * g
            tv = jnp.tanh(coeff * (g + 0.044715 * (g2_ * g)))
            val = 0.5 * g * (1.0 + tv)
            slope = 0.5 * (1.0 + tv) + 0.5 * g * (1.0 - tv * tv) * (
                coeff * (1.0 + 3.0 * 0.044715 * g2_)
            )
            V[rows, :] = val
            U[rows, :] = u * slope
            G[rows, :] = (val * u).astype(BF16)

    contract = (((0,), (0,)), ((), ()))

    def lowd():
        for j in range(3):
            r = lax.dot_general(
                Pb[:, 2 * RANK : 3 * RANK], G[:, j * CH : (j + 1) * CH], contract,
                preferred_element_type=F32,
            )
            for i in range(3):
                L[3 * j + i] = r[:, i * 128 : (i + 1) * 128].reshape(8, 2, 16, 128)

    def chunk(j, side):
        cols = slice(j * CH, (j + 1) * CH)
        row0 = (xl if side == 0 else xo) * 256
        part = pl.ds(pl.multiple_of(row0, 256), 256)
        H[...] = lax.dot_general(
            Y[part, :], w[cols, :], (((1,), (1,)), ((), ())), preferred_element_type=F32
        )

        @pl.loop(0, 8)
        def _(i):
            rows = pl.ds(pl.multiple_of(i * 32, 32), 32)
            from_ = pl.ds(pl.multiple_of(row0 + i * 32, 32), 32)
            h = H[rows, :]
            GG[rows, :] = (h * U[from_, cols]).astype(BF16)
            UG[rows, :] = (h * V[from_, cols]).astype(BF16)

        for k, ref in enumerate((GG, UG)):
            r = lax.dot_general(
                Pb[part, k * RANK : (k + 1) * RANK], ref[...], contract,
                preferred_element_type=F32,
            )
            for i in range(3):
                tile = r[:, i * 128 : (i + 1) * 128].reshape(8, 2, 16, 128)
                g = 9 + 6 * j + 3 * k + i
                L[g] = tile if side == 0 else L[g] + tile

    def gdrain():
        for p in range(2):
            shards(p, 15, gs.at[p])
        part = RA.at[pl.ds(0, 15)]
        pltpu.make_async_copy(part, part, ras).wait()
        pltpu.make_async_copy(part, part, rcs).wait()

    def mdrain():
        @pl.when(d < 15)
        def _():
            part = MS.at[pl.ds(0, 14)]
            pltpu.make_async_copy(part, part, ms).wait()
            part = TS.at[pl.ds(0, 15)]
            pltpu.make_async_copy(part, part, ts).wait()

        @pl.when(d == 15)
        def _():
            pltpu.make_async_copy(MS, MS, ms).wait()

    def rdrain():
        pltpu.make_async_copy(rsend, rsend, rs).wait()
        pltpu.make_async_copy(xsend, xsend, xs).wait()
        pltpu.make_async_copy(OUT, OUT, ld.at[9]).wait()

    act(0, 32)
    gmirror(0, range(7))
    g3(0, 0)
    g3(0, 1)
    lowd()
    rnd(0, 0)
    rnd(1, 0)
    gpair(1)
    rsend1()
    gmirror(1, (1, 2))
    gfar(1)
    msend(1 - xh)
    rnd(0, 1)
    rnd(1, 1)
    loads[6].wait()
    g3(1, 0)
    chunk(0, 0)
    gmirror(1, (4, 5))
    chunk(1, 0)
    rsum()
    gmirror(1, (6,))
    chunk(2, 0)
    g3(1, 1)
    chunk(0, 1)
    xout(2)
    rnd(0, 2)
    rnd(1, 2)
    chunk(1, 1)
    rnd(3, 0)
    chunk(2, 1)
    rnd(4, 0)
    turn()
    tsend(0, 4)
    rnd(3, 1)
    xin(2)
    rnd(2, 0)
    rnd(4, 1)
    tsend(4, 8)
    rnd(3, 2)
    rnd(2, 1)
    rnd(4, 2)
    tsend(8, 12)
    fin(0)
    fin(1)
    rnd(2, 2)
    tsend(12, 16)
    fin(3)
    gdrain()
    mdrain()
    last(0)
    last(1)
    fin(4)
    last(3)
    fin(2)
    back()
    last(4)
    rdrain()


def on_device(inputs, out_grad, gate_pre, up_pre, w_down, proj_new, proj_old, first_old, second_old):
    flip = lambda a: jnp.transpose(a, (1, 0, 2))
    shape = jax.ShapeDtypeStruct((3, 16, C), F32)
    dma = pltpu.SemaphoreType.DMA
    low, turned_first, turned_second = pl.pallas_call(
        kernel,
        out_shape=(shape,) * 3,
        in_specs=[pl.BlockSpec(memory_space=pl.ANY)] * 9,
        out_specs=(pl.BlockSpec(memory_space=pl.ANY),) * 3,
        scratch_shapes=[
            pltpu.VMEM((SH, D), BF16),
            pltpu.VMEM((TOK, D), BF16),
            pltpu.VMEM((TOK, 3 * RANK), BF16),
            pltpu.VMEM((SLAB, RANK), BF16),
            pltpu.VMEM((TOK, C), BF16),
            pltpu.VMEM((TOK, C), BF16),
            pltpu.VMEM((C, D), BF16),
            pltpu.VMEM((3, D, RANK), BF16),
            pltpu.VMEM((3, 16, C), F32),
            pltpu.VMEM((3, 16, C), F32),
            pltpu.VMEM((TOK, C), F32),
            pltpu.VMEM((TOK, C), F32),
            pltpu.VMEM((TOK, C), BF16),
            pltpu.VMEM((256, CH), F32),
            pltpu.VMEM((256, CH), BF16),
            pltpu.VMEM((256, CH), BF16),
            pltpu.VMEM((27, 8, 2, 16, 128), F32),
            pltpu.VMEM((RANK, RANK), F32),
            pltpu.VMEM((2, RANK, RANK), F32),
            pltpu.VMEM((2, RANK, RANK), F32),
            pltpu.VMEM((15, 72, 128), BF16),
            pltpu.VMEM((16, 72, 128), BF16),
            pltpu.VMEM((16, 72, 128), BF16),
            pltpu.VMEM((15, 72, 128), BF16),
            pltpu.VMEM((27, 32, 128), F32),
            pltpu.VMEM((9, 16, C), F32),
            pltpu.VMEM((16, 40, 128), BF16),
            pltpu.VMEM((16, 40, 128), BF16),
            pltpu.VMEM((40, 128), BF16),
            pltpu.VMEM((16, 40, 128), BF16),
            pltpu.VMEM((7, ROWS, 128), BF16),
            pltpu.VMEM((7, ROWS, 128), BF16),
            pltpu.VMEM((XROWS, 128), BF16),
            pltpu.VMEM((XROWS, 128), BF16),
            dma((12,)), dma((2,)), dma((2, 9)), dma, dma, dma, dma,
            dma, dma((NQ, 7)), dma, dma((NQ,)), dma, dma, dma, dma,
        ],
        compiler_params=pltpu.CompilerParams(
            collective_id=0, has_side_effects=True, vmem_limit_bytes=63 * 1024 * 1024
        ),
    )(
        inputs, out_grad, gate_pre, up_pre, w_down, flip(proj_new), flip(proj_old),
        flip(first_old), flip(second_old),
    )
    first = 0.9 * turned_first + 0.1 * low
    second = 0.999 * turned_second + 0.001 * low * low
    return flip(first), flip(second)


def solution(mesh):
    placed = (
        P(("dp", "tensor"), None),
        P(("dp", "tensor"), None),
        P("dp", "tensor"),
        P("dp", "tensor"),
        P("tensor", None),
        P(),
        P("tensor", None, None),
        P("dp", None, "tensor"),
        P("dp", None, "tensor"),
    )
    return jax.shard_map(
        on_device,
        mesh=mesh,
        in_specs=placed,
        out_specs=(P("dp", None, "tensor"), P("dp", None, "tensor")),
        check_vma=False,
    )
```

```python
import jax
import jax.numpy as jnp
from jax import lax
from jax.experimental import pallas as pl
from jax.experimental.pallas import tpu as pltpu
from jax.sharding import PartitionSpec as P

coeff = 0.7978845608028654
F32 = jnp.float32
BF16 = jnp.bfloat16
D = 2304
C = 1152
TOK = 512
SH = 32
RANK = 256
SLAB = 144
CH = 384
QT0 = (0, 5, 9, 15, 21)
QN = (5, 4, 6, 6, 6)
NQ = 5
XF = (False, False, True, False, False)
CR = tuple(16 if f else 32 for f in XF)
XR = tuple(128 if f else 16 for f in XF)
OFF = tuple(sum(QN[i] * CR[i] + 8 for i in range(q)) for q in range(NQ + 1))
XOFF = tuple(sum(QN[i] * XR[i] + 8 for i in range(q)) for q in range(NQ + 1))
ROWS = OFF[NQ]
XROWS = XOFF[NQ]
BACK = (0, 2, 1, 3, 5, 4, 6)
TOP = 181.0
MESH = pl.DeviceIdType.MESH


def top_of(x):
    top = jnp.max(jnp.max(jnp.abs(x), axis=0), axis=0, keepdims=True)
    return jnp.broadcast_to(jnp.maximum(top, 1e-30), (8, 128)).astype(BF16)


def code(x, top):
    n, rows, _ = x.shape
    u = x * (TOP / top.astype(F32))[0:1][None]
    u2 = u * u
    u4 = u2 * u2
    u8 = u4 * u4
    return ((u8 * u4) * (u2 * (u * jnp.abs(u)))).astype(BF16).reshape(n * rows, 128)


def value(v, scale, n):
    v = v.astype(F32)
    r = jnp.exp2(jnp.log2(jnp.abs(v)) * 0.0625)
    return (jnp.where(v < 0.0, -r, r) * (scale * (1.0 / TOP))).reshape(n, -1, 128)


def enc(x, buf):
    n, rows, _ = x.shape
    top = top_of(x)
    buf[pl.ds(n * rows, 8)] = top
    buf[pl.ds(0, n * rows)] = code(x, top)


def dec(buf, n, rows):
    scale = buf[pl.ds(n * rows, 8)].astype(F32)[0:1]
    return value(buf[pl.ds(0, n * rows)], scale, n)


def enc2(a, b, buf):
    ta, tb = top_of(a), top_of(b)
    first = lax.broadcasted_iota(jnp.int32, (8, 128), 0) < 4
    buf[pl.ds(64, 8)] = jnp.where(first, ta.astype(F32), tb.astype(F32)).astype(BF16)
    buf[pl.ds(0, 32)] = code(a, ta)
    buf[pl.ds(32, 32)] = code(b, tb)


def dec2(buf):
    scale = buf[pl.ds(64, 8)].astype(F32)
    return value(buf[pl.ds(0, 32)], scale[0:1], 2), value(buf[pl.ds(32, 32)], scale[4:5], 2)


def kernel(
    inp_h, og_h, gate_h, up_h, w_h, pn_h, po_h, fo_h, so_h,
    low_h, tf_h, ts_h,
    inp, Y, Pb, po, gate, up, w, pn, fo, so, V, U, G, H, GG, UG, L, R, M, T, MS, MR, TS, TB, FIN, OUT, RA, RB, RC, RD,
    rsend, rrecv, xsend, xrecv,
    ld, gs, gr, ms, mr, ts, tr, rs, rr, xs, xr, ras, rar, rcs, rcr,
):
    d = lax.axis_index("dp")
    t = lax.axis_index("tensor")
    z = d // 2
    xh = lax.rem(d, 2)
    c = lax.rem(t, 2)
    y = lax.rem(t // 2, 4)
    xl = t // 8
    kd = jnp.minimum(d // 5, 2)

    def tid(a, b):
        return a * 8 + b * 2 + c

    yn = lax.rem(y + 1, 4)
    yb = lax.rem(y + 3, 4)
    y2 = lax.rem(y + 2, 4)
    xo = 1 - xl
    sib = t + 1 - 2 * c
    xp = tid(xo, y)
    yp = tid(xl, yn)
    ym = tid(xl, yb)
    zn = lax.rem(z + 1, 8)
    zb = lax.rem(z + 7, 8)
    zlong = jnp.where(c == 0, zn, zb)
    zshort = jnp.where(c == 0, zb, zn)
    dlong = zlong * 2 + xh
    dshort = zshort * 2 + xh
    dfar = lax.rem(z + 8 + 2 * (1 - 2 * c), 8) * 2 + xh
    dx = d + 1 - 2 * xh
    step = 1 - 2 * c

    def loc(src, dst, i):
        return pltpu.make_async_copy(src, dst, ld.at[i])

    own = pl.ds(pl.multiple_of(t * SH, SH), SH)
    loads = [
        loc(og_h, Y.at[own], 0),
        loc(inp_h, inp, 1),
        loc(pn_h.at[2], pn.at[2], 2),
        loc(po_h.at[kd], po, 3),
        loc(gate_h, gate, 4),
        loc(up_h, up, 5),
        loc(w_h, w, 6),
        loc(fo_h, fo, 7),
        loc(so_h, so, 8),
        loc(pn_h.at[0], pn.at[0], 10),
        loc(pn_h.at[1], pn.at[1], 11),
    ]
    for i in (0, 2, 1, 9, 10, 7, 8, 3):
        loads[i].start()

    bar = pltpu.get_barrier_semaphore()
    lane = (xp, yp, ym, tid(xl, y2), tid(xo, yn), tid(xo, yb), tid(xo, y2))

    @pl.loop(1, 16)
    def _(j):
        pl.semaphore_signal(
            bar, inc=1, device_id={"tensor": lax.rem(t + j, 16)}, device_id_type=MESH
        )
        pl.semaphore_signal(
            bar, inc=1, device_id={"dp": lax.rem(d + j, 16)}, device_id_type=MESH
        )

    pay = ((Pb, SH, SH), (Y, SH, SH))

    def gcopy(p, slot, target, i):
        buf, rows, mult = pay[p]
        sl = pl.ds(pl.multiple_of(slot * rows, mult), rows)
        return pltpu.make_async_remote_copy(
            src_ref=buf.at[sl], dst_ref=buf.at[sl], send_sem=gs.at[p],
            recv_sem=gr.at[p, i], device_id={"tensor": target}, device_id_type=MESH,
        )

    def gsend(p, slot, target, i):
        gcopy(p, slot, target, i).start()

    def gwait(p, j):
        gcopy(p, lane[j], sib, j).wait_recv()

    def shards(p, n, sem):
        buf, rows, _ = pay[p]
        part = buf.at[pl.ds(0, n * rows)]
        pltpu.make_async_copy(part, part, sem).wait()

    def project():
        for a in (0, 2, 1, 9, 10):
            loads[a].wait()
            if a in (0, 1):
                continue
            k = (2, 0, 1)[(2, 9, 10).index(a)]
            lhs = inp[...] if k < 2 else Y[own, :]
            Pb[own, k * RANK : (k + 1) * RANK] = jnp.dot(
                lhs, pn[k], preferred_element_type=F32
            ).astype(BF16)
        for i in (4, 5, 6):
            loads[i].start()

    def gown(p, n):
        for j in range(n):
            gsend(p, t, lane[j], BACK[j])
        gsend(p, t, sib, 7)

    def gmirror(p, js):
        for j in js:
            gwait(p, j)
            gsend(p, lane[j], sib, 7 if j in (1, 2, 3) else 8)

    def gpair(p):
        gwait(p, 0)
        gsend(p, xp, yp, 5)
        gsend(p, xp, ym, 4)
        gsend(p, xp, sib, 8)

    def gfar(p):
        gwait(p, 3)
        gsend(p, lane[3], xp, 6)
        gsend(p, lane[3], sib, 7)

    def g3(p, side):
        shards(p, 4, gr.at[p, 7 + side])

    def rpart():
        loads[3].wait()
        slab = pl.ds(pl.multiple_of(t * SLAB, 16), SLAB)
        R[...] = lax.dot_general(
            pn[kd, slab, :], po[...], (((0,), (0,)), ((), ())), preferred_element_type=F32
        )
        for j in range(16):
            rows = slice(16 * j, 16 * j + 16)
            enc(jnp.stack([R[rows, 0:128], R[rows, 128:256]]), RA.at[j])

    def spread(src, dst, ssem, rsem):
        @pl.loop(1, 16)
        def _(i):
            j = lax.rem(t + i, 16)
            pltpu.make_async_remote_copy(
                src_ref=src(j), dst_ref=dst, send_sem=ssem, recv_sem=rsem,
                device_id={"tensor": j}, device_id_type=MESH,
            ).start()

        pltpu.make_async_copy(src(t), dst, rsem).start()

    def rsend1():
        spread(lambda j: RA.at[j], RB.at[t], ras, rar)

    def rsum():
        pltpu.make_async_copy(RB, RB, rar).wait()
        x = dec(RB.at[0], 2, 16)
        for j in range(1, 16):
            x = x + dec(RB.at[j], 2, 16)
        enc(x, RC)
        spread(lambda j: RC, RD.at[t], rcs, rcr)

    def mrem(o):
        return pltpu.make_async_remote_copy(
            src_ref=MS.at[o], dst_ref=MR.at[d], send_sem=ms, recv_sem=mr,
            device_id={"dp": o}, device_id_type=MESH,
        )

    def menc():
        loads[7].wait()
        loads[8].wait()
        for o in range(15):
            c0 = min((o % 5) * 256, 896)
            pair = [
                jnp.stack([ref[o // 5, :, c0 + i * 128 : c0 + i * 128 + 128] for i in range(2)])
                for ref in (fo, so)
            ]
            enc2(*pair, MS.at[o])

    def msend(par):
        @pl.loop(0, 8)
        def _(j):
            o = 2 * j + par

            @pl.when(jnp.logical_and(o < 15, o != d))
            def _():
                mrem(o).start()

            @pl.when(jnp.logical_and(o < 15, o == d))
            def _():
                pltpu.make_async_copy(MS.at[o], MR.at[d], mr).start()

    def trem(dst):
        return pltpu.make_async_remote_copy(
            src_ref=TS.at[dst], dst_ref=TB.at[d], send_sem=ts, recv_sem=tr,
            device_id={"dp": dst}, device_id_type=MESH,
        )

    def turn():
        pltpu.make_async_copy(RD, RD, rcr).wait()

        @pl.when(d < 15)
        def _():
            pltpu.make_async_copy(MR, MR, mr).wait()

            @pl.loop(0, 16)
            def _(s):
                rows = pl.ds(pl.multiple_of(s * 16, 16), 16)
                for m, x in enumerate(dec2(MR.at[s])):
                    M[m, rows, 0:128] = x[0]
                    M[m, rows, 128:256] = x[1]

            for j in range(16):
                x = dec(RD.at[j], 2, 16)
                R[16 * j : 16 * j + 16, 0:128] = x[0]
                R[16 * j : 16 * j + 16, 128:256] = x[1]
            rot = R[...]
            for m in range(2):
                T[m] = jnp.dot(
                    rot if m == 0 else rot * rot, M[m],
                    precision=lax.Precision.HIGHEST, preferred_element_type=F32,
                )

    def tsend(lo, hi):
        @pl.when(d < 15)
        def _():
            @pl.loop(lo, hi)
            def _(i):
                j = lax.rem(d + i, 16)
                rows = pl.ds(pl.multiple_of(j * 16, 16), 16)
                pair = [jnp.stack([T[m, rows, 0:128], T[m, rows, 128:256]]) for m in range(2)]
                enc2(*pair, TS.at[j])

                @pl.when(i > 0)
                def _():
                    trem(j).start()

                @pl.when(i == 0)
                def _():
                    pltpu.make_async_copy(TS.at[j], TB.at[d], tr).start()

    def span(q):
        return pl.ds(OFF[q], OFF[q + 1] - OFF[q])

    def xspan(q):
        return pl.ds(XOFF[q], XOFF[q + 1] - XOFF[q])

    def rcopy(q, i):
        sp = span(q)
        return pltpu.make_async_remote_copy(
            src_ref=rsend.at[i, sp], dst_ref=rrecv.at[i, sp], send_sem=rs, recv_sem=rr.at[q, i],
            device_id={"dp": dlong if i < 3 else dshort if i < 6 else dfar}, device_id_type=MESH,
        )

    def mine(q, zdest):
        tiles = pl.ds(QT0[q], QN[q])
        if XF[q]:
            return L[tiles, zdest, xh]
        return L[tiles, zdest].reshape(QN[q], 32, 128)

    def rnd(q, r):
        n = QN[q]
        tiles = span(q)
        for i, far in ((6, 4), (r, step * (3 - r)), (3 + r, -step * (3 - r))):
            if i == 6 and r > 0:
                continue
            x = mine(q, lax.rem(z + 8 + far, 8))
            if r > 0:
                rcopy(q, i - 1).wait_recv()
                x = x + dec(rrecv.at[i - 1, tiles], n, CR[q])
            if i == 1:
                rcopy(q, 6).wait_recv()
                x = x + dec(rrecv.at[6, tiles], n, CR[q])
            enc(x, rsend.at[i, tiles])
            rcopy(q, i).start()

    def xcopy(q):
        sp = xspan(q)
        return pltpu.make_async_remote_copy(
            src_ref=xsend.at[sp], dst_ref=xrecv.at[sp], send_sem=xs, recv_sem=xr.at[q],
            device_id={"dp": dx}, device_id_type=MESH,
        )

    def xout(q):
        n = QN[q]
        x = L[pl.ds(QT0[q], n), :, 1 - xh]
        enc(x.reshape(n, 128, 128), xsend.at[xspan(q)])
        xcopy(q).start()

    def xin(q):
        n = QN[q]
        tiles = pl.ds(QT0[q], n)
        xcopy(q).wait_recv()
        x = dec(xrecv.at[xspan(q)], n, 128)
        L[tiles, :, xh] = L[tiles, :, xh] + x.reshape(n, 8, 16, 128)

    def emit(q, low):
        n = QN[q]
        for i in range(n):
            g = QT0[q] + i
            k, ct = (2, g) if g < 9 else ((g - 9) % 6 // 3, (g - 9) // 6 * 3 + (g - 9) % 3)
            OUT[k, :, ct * 128 : (ct + 1) * 128] = low[i]
        if q < 2:
            part = (2, slice(None), pl.ds(QT0[q] * 128, n * 128))
        else:
            part = (pl.ds(0, 2), slice(None), pl.ds((q - 2) * CH, CH))
        pltpu.make_async_copy(OUT.at[part], low_h.at[part], ld.at[9]).start()

    def fin(q):
        n = QN[q]
        tiles = span(q)
        dst = pl.ds(QT0[q], n)
        rcopy(q, 2).wait_recv()
        rcopy(q, 5).wait_recv()
        x = mine(q, z) + dec(rrecv.at[2, tiles], n, CR[q]) + dec(rrecv.at[5, tiles], n, CR[q])
        if XF[q]:
            emit(q, x)
            return
        FIN[dst] = x
        enc(FIN[dst, pl.ds(pl.multiple_of((1 - xh) * 16, 16), 16), :], xsend.at[xspan(q)])
        xcopy(q).start()

    def last(q):
        n = QN[q]
        dst = pl.ds(QT0[q], n)
        xcopy(q).wait_recv()
        emit(
            q,
            FIN[dst, pl.ds(pl.multiple_of(xh * 16, 16), 16), :]
            + dec(xrecv.at[xspan(q)], n, 16),
        )

    def back():
        pltpu.make_async_copy(TB, TB, tr).wait()
        for o in range(15):
            for m, x in enumerate(dec2(TB.at[o])):
                for i in range(2):
                    ct = min(2 * (o % 5), 7) + i
                    if o % 5 < 4 or i == 1:
                        OUT[3 + 3 * m + o // 5, :, ct * 128 : (ct + 1) * 128] = x[i]
        loc(OUT.at[pl.ds(3, 3)], tf_h, 9).start()
        loc(OUT.at[pl.ds(6, 3)], ts_h, 9).start()

    project()
    pl.semaphore_wait(bar, 30)
    gown(0, 7)
    gown(1, 4)
    menc()
    msend(xh)
    rpart()
    loads[4].wait()
    loads[5].wait()

    def act(lo, hi):
        @pl.loop(lo, hi)
        def _(i):
            rows = pl.ds(pl.multiple_of(i * 16, 16), 16)
            g = gate[rows, :].astype(F32)
            u = up[rows, :].astype(F32)
            g2_ = g * g
            tv = jnp.tanh(coeff * (g + 0.044715 * (g2_ * g)))
            val = 0.5 * g * (1.0 + tv)
            slope = 0.5 * (1.0 + tv) + 0.5 * g * (1.0 - tv * tv) * (
                coeff * (1.0 + 3.0 * 0.044715 * g2_)
            )
            V[rows, :] = val
            U[rows, :] = u * slope
            G[rows, :] = (val * u).astype(BF16)

    contract = (((0,), (0,)), ((), ()))

    def lowd():
        for j in range(3):
            r = lax.dot_general(
                Pb[:, 2 * RANK : 3 * RANK], G[:, j * CH : (j + 1) * CH], contract,
                preferred_element_type=F32,
            )
            for i in range(3):
                L[3 * j + i] = r[:, i * 128 : (i + 1) * 128].reshape(8, 2, 16, 128)

    def chunk(j, side):
        cols = slice(j * CH, (j + 1) * CH)
        row0 = (xl if side == 0 else xo) * 256
        part = pl.ds(pl.multiple_of(row0, 256), 256)
        H[...] = lax.dot_general(
            Y[part, :], w[cols, :], (((1,), (1,)), ((), ())), preferred_element_type=F32
        )

        @pl.loop(0, 8)
        def _(i):
            rows = pl.ds(pl.multiple_of(i * 32, 32), 32)
            from_ = pl.ds(pl.multiple_of(row0 + i * 32, 32), 32)
            h = H[rows, :]
            GG[rows, :] = (h * U[from_, cols]).astype(BF16)
            UG[rows, :] = (h * V[from_, cols]).astype(BF16)

        for k, ref in enumerate((GG, UG)):
            r = lax.dot_general(
                Pb[part, k * RANK : (k + 1) * RANK], ref[...], contract,
                preferred_element_type=F32,
            )
            for i in range(3):
                tile = r[:, i * 128 : (i + 1) * 128].reshape(8, 2, 16, 128)
                g = 9 + 6 * j + 3 * k + i
                L[g] = tile if side == 0 else L[g] + tile

    def gdrain():
        for p in range(2):
            shards(p, 15, gs.at[p])
        part = RA.at[pl.ds(0, 15)]
        pltpu.make_async_copy(part, part, ras).wait()
        pltpu.make_async_copy(part, part, rcs).wait()

    def mdrain():
        @pl.when(d < 15)
        def _():
            part = MS.at[pl.ds(0, 14)]
            pltpu.make_async_copy(part, part, ms).wait()
            part = TS.at[pl.ds(0, 15)]
            pltpu.make_async_copy(part, part, ts).wait()

        @pl.when(d == 15)
        def _():
            pltpu.make_async_copy(MS, MS, ms).wait()

    def rdrain():
        pltpu.make_async_copy(rsend, rsend, rs).wait()
        pltpu.make_async_copy(xsend, xsend, xs).wait()
        pltpu.make_async_copy(OUT, OUT, ld.at[9]).wait()

    act(0, 32)
    gmirror(0, range(7))
    g3(0, 0)
    g3(0, 1)
    lowd()
    rnd(0, 0)
    rnd(1, 0)
    gpair(1)
    rsend1()
    gmirror(1, (1, 2))
    gfar(1)
    msend(1 - xh)
    rnd(0, 1)
    rnd(1, 1)
    loads[6].wait()
    g3(1, 0)
    chunk(0, 0)
    gmirror(1, (4, 5))
    chunk(1, 0)
    rsum()
    gmirror(1, (6,))
    chunk(2, 0)
    g3(1, 1)
    chunk(0, 1)
    xout(2)
    rnd(0, 2)
    rnd(1, 2)
    chunk(1, 1)
    rnd(3, 0)
    chunk(2, 1)
    rnd(4, 0)
    turn()
    tsend(0, 4)
    rnd(3, 1)
    xin(2)
    rnd(2, 0)
    rnd(4, 1)
    tsend(4, 8)
    rnd(3, 2)
    rnd(2, 1)
    rnd(4, 2)
    tsend(8, 12)
    fin(0)
    fin(1)
    tsend(12, 16)
    rnd(2, 2)
    fin(3)
    fin(4)
    last(0)
    last(1)
    last(3)
    fin(2)
    back()
    gdrain()
    mdrain()
    last(4)
    rdrain()


def on_device(inputs, out_grad, gate_pre, up_pre, w_down, proj_new, proj_old, first_old, second_old):
    flip = lambda a: jnp.transpose(a, (1, 0, 2))
    shape = jax.ShapeDtypeStruct((3, 16, C), F32)
    dma = pltpu.SemaphoreType.DMA
    low, turned_first, turned_second = pl.pallas_call(
        kernel,
        out_shape=(shape,) * 3,
        in_specs=[pl.BlockSpec(memory_space=pl.ANY)] * 9,
        out_specs=(pl.BlockSpec(memory_space=pl.ANY),) * 3,
        scratch_shapes=[
            pltpu.VMEM((SH, D), BF16),
            pltpu.VMEM((TOK, D), BF16),
            pltpu.VMEM((TOK, 3 * RANK), BF16),
            pltpu.VMEM((SLAB, RANK), BF16),
            pltpu.VMEM((TOK, C), BF16),
            pltpu.VMEM((TOK, C), BF16),
            pltpu.VMEM((C, D), BF16),
            pltpu.VMEM((3, D, RANK), BF16),
            pltpu.VMEM((3, 16, C), F32),
            pltpu.VMEM((3, 16, C), F32),
            pltpu.VMEM((TOK, C), F32),
            pltpu.VMEM((TOK, C), F32),
            pltpu.VMEM((TOK, C), BF16),
            pltpu.VMEM((256, CH), F32),
            pltpu.VMEM((256, CH), BF16),
            pltpu.VMEM((256, CH), BF16),
            pltpu.VMEM((27, 8, 2, 16, 128), F32),
            pltpu.VMEM((RANK, RANK), F32),
            pltpu.VMEM((2, RANK, RANK), F32),
            pltpu.VMEM((2, RANK, RANK), F32),
            pltpu.VMEM((15, 72, 128), BF16),
            pltpu.VMEM((16, 72, 128), BF16),
            pltpu.VMEM((16, 72, 128), BF16),
            pltpu.VMEM((15, 72, 128), BF16),
            pltpu.VMEM((27, 32, 128), F32),
            pltpu.VMEM((9, 16, C), F32),
            pltpu.VMEM((16, 40, 128), BF16),
            pltpu.VMEM((16, 40, 128), BF16),
            pltpu.VMEM((40, 128), BF16),
            pltpu.VMEM((16, 40, 128), BF16),
            pltpu.VMEM((7, ROWS, 128), BF16),
            pltpu.VMEM((7, ROWS, 128), BF16),
            pltpu.VMEM((XROWS, 128), BF16),
            pltpu.VMEM((XROWS, 128), BF16),
            dma((12,)), dma((2,)), dma((2, 9)), dma, dma, dma, dma,
            dma, dma((NQ, 7)), dma, dma((NQ,)), dma, dma, dma, dma,
        ],
        compiler_params=pltpu.CompilerParams(
            collective_id=0, has_side_effects=True, vmem_limit_bytes=63 * 1024 * 1024
        ),
    )(
        inputs, out_grad, gate_pre, up_pre, w_down, flip(proj_new), flip(proj_old),
        flip(first_old), flip(second_old),
    )
    first = 0.9 * turned_first + 0.1 * low
    second = 0.999 * turned_second + 0.001 * low * low
    return flip(first), flip(second)


def solution(mesh):
    placed = (
        P(("dp", "tensor"), None),
        P(("dp", "tensor"), None),
        P("dp", "tensor"),
        P("dp", "tensor"),
        P("tensor", None),
        P(),
        P("tensor", None, None),
        P("dp", None, "tensor"),
        P("dp", None, "tensor"),
    )
    return jax.shard_map(
        on_device,
        mesh=mesh,
        in_specs=placed,
        out_specs=(P("dp", None, "tensor"), P("dp", None, "tensor")),
        check_vma=False,
    )
```
